32 devices in a mesh: gx: 4 (over y, core), yz: 8 (over z, x).
Axes of the slice: x: 2, y: 2, z: 4, core: 2. Of those that a mesh axis runs over, the one named last changes fastest.
Arguments:
- flow_speed_field: float32 [3, 32, 64, 128], P(None, 'gx', 'yz'), may hold values from -6 to 6
- thermal_field: float32 [32, 64, 128], P('gx', 'yz'), may hold values from 0.5 to 2
- walker_speed_vectors: float32 [3, 4096, 128], P(None, ('gx', 'yz')), may hold values from -6 to 6
- walker_statistical_mass: float32 [4096, 128], P(('gx', 'yz')), may hold values from 0.5 to 2
- gaussian_samples: float32 [2, 3, 4096, 128], P(None, None, ('gx', 'yz')), may hold values from -6 to 6
- walker_strip_position: int32 [4096, 128], P(('gx', 'yz')), may hold values from 0 to 127
- group_active_tally: int32 [4096], P(('gx', 'yz')), may hold values from 32 to 128
- group_resident_strip: int32 [4096], P(('gx', 'yz')), may hold values from 0 to 63
- migrating_group_table: int32 [512], P(('gx', 'yz')), may hold values from 0 to 127, as said below
- target_processor_slot: int32 [512, 1], P(('gx', 'yz')), may hold values from 0 to 7; in each aligned block of 16 rows (0 to 15, 16 to 31, ...) at most 4 rows name the same one
- entered_strip_slot: int32 [512], P(('gx', 'yz')), may hold values from 0 to 63
Outputs:
- new_fields: float32 [4, 32, 64, 128], P(None, 'gx', 'yz')
- particle_velocity: float32 [3, 4096, 128], P(None, ('gx', 'yz'))
The draws below stay inside these ranges and needn't reach their ends.
Inputs may be any that keep to these rules, and one draw needn't show every extreme that they name: `migrating_group_table`: within each device's 16 entries the block indices are distinct. `target_processor_slot`: among the 16 rows of one device no yz index appears more than 4 times.
All inputs are finite; a program needn't handle non-finite values.
Results may differ from the reference program's by a relative error of at most 0.00005.
Values sent between devices are 32-bit elements; how exact they have to be, the bound alone decides.
A program may use at most 64 MiB of HBM per device.

```python
import math
import jax
import jax.numpy as jnp
import numpy as np
from jax import lax

CX = 8
CY = 8
CZ = 128
SLOTS = 128
BLK_DEV = 128
MIG_DEV = 16
CAP = 4
PENCILS = 64
GRID_SPAN_X = 32
GRID_SPAN_Y = 64
GRID_SPAN_Z = 128
NBLK = 4096
MIGS = 512
N_GX = 4
N_YZ = 8


def draw_migrating_group_table(key, part):
    keys = jax.random.split(key, N_GX * N_YZ)

    def pick(single):
        return jax.random.permutation(single, BLK_DEV)[:MIG_DEV].astype(jnp.int32)
    return jax.vmap(pick)(keys).reshape(-1)


def touch_ends(entries, stream_key, low, largest):
    extent = entries.shape
    spot = [jax.random.randint(jax.random.fold_in(stream_key, axis), (), 0, extent[axis]) for axis in range(len(extent))]
    entries = entries.at[tuple(spot)].set(low)
    longest = extent.index(max(extent))
    spot[longest] = (spot[longest] + 1) % extent[longest]
    return entries.at[tuple(spot)].set(largest)


def block_levels(stream_key, shape, shards, low, largest):
    level = 1.0
    for dim, shards_of in shards:
        heights = jax.random.uniform(jax.random.fold_in(jax.random.fold_in(stream_key, 6), dim), (shards_of,), jnp.float32, low / len(shards), largest / len(shards))
        level = level * jnp.repeat(jnp.exp(heights), shape[dim] // shards_of).reshape((-1,) + (1,) * (len(shape) - 1 - dim))
    return level


def deal_out(stream_key, own, number, rows, amount, top, limit, lean):
    sequence = jax.random.permutation(stream_key, amount)
    packed, ordinary = load_shares(amount, rows * top, limit, lean, True), load_shares(amount, rows * top, limit, lean, False)
    places = jnp.arange(amount)

    def named(sizes, offset_by):
        used = int((sizes > 0).sum())
        fixed = max(1, used // 4)
        shifted = fixed + (places - fixed + offset_by * (used - fixed)) % max(1, amount - fixed)
        return jnp.zeros((amount,), jnp.int32).at[sequence[jnp.where(places < fixed, places, shifted)]].set(jnp.asarray(sizes, jnp.int32))

    sizes = jnp.where(number % 4 == 0, named(packed, number // 4), named(ordinary, number - number // 4 - 1))
    mixed = jax.random.permutation(jax.random.fold_in(own, 3), amount)
    giver, sink = mixed[0:amount // 2 * 2:2], mixed[1:amount // 2 * 2:2]
    slack = jnp.minimum(sizes[giver] - 1, limit - sizes[sink]) // 2
    slack = jnp.where((giver == sequence[0]) | (sink == sequence[0]) | (sizes[sink] == 0), 0, jnp.maximum(slack, 0))
    shifted = jax.random.randint(jax.random.fold_in(own, 4), (amount // 2,), 0, 1 << 20) % (slack + 1)
    sizes = sizes.at[giver].add(-shifted).at[sink].add(shifted)
    items = jnp.searchsorted(jnp.cumsum(sizes), jnp.arange(rows * top), side="right").astype(jnp.int32)
    grid = items.reshape(top, rows).T
    grid = grid[jax.random.permutation(jax.random.fold_in(own, 1), rows)]
    offset_by = jax.random.randint(jax.random.fold_in(own, 2), (rows, 1), 0, top)
    return jnp.take_along_axis(grid, (jnp.arange(top)[None, :] + offset_by) % top, axis=1)


def load_shares(number_of, total, limit, skew, full):
    loads = [(1 << 20) // math.isqrt(grade ** skew) + 1 for grade in range(1, number_of + 1)]
    largest = limit if full else min(limit, max(-(-total // number_of), total * loads[0] // sum(loads)))
    least = 1 if total - largest >= number_of - 1 else 0
    holding, surplus = [largest] + [least] * (number_of - 1), total - largest - least * (number_of - 1)
    while surplus > 0:
        movable = [i for i in range(1, number_of) if holding[i] < largest] or [i for i in range(1, number_of) if holding[i] < limit]
        pool, left = sum([loads[i] for i in movable]), surplus
        for i in movable:
            more = min(limit - holding[i], max(1, left * loads[i] // pool), surplus)
            holding[i] = holding[i] + more
            surplus = surplus - more
    return np.array(holding)


def centred(own_key, dims, spread, bound, cuts=(), kind=jnp.bfloat16):
    entries = spread * jax.random.normal(own_key, dims, jnp.float32)
    if cuts:
        entries = entries * block_levels(own_key, dims, cuts, -0.22, 0.18)
    return jnp.clip(entries, -bound, bound).astype(kind)


def setup_inputs(seed: int = 0) -> dict:
    arg_keys = jax.random.split(jax.random.key(seed), 12)
    flow_speed_field = centred(arg_keys[0], (3, GRID_SPAN_X, GRID_SPAN_Y, GRID_SPAN_Z), 1.0, 6.0, ((1, 4), (2, 8)), jnp.float32)
    thermal_field = jnp.clip(jnp.exp(math.log(2.0) - 1.3862944 * jax.random.uniform(arg_keys[1], (GRID_SPAN_X, GRID_SPAN_Y, GRID_SPAN_Z), jnp.float32) ** block_levels(arg_keys[1], (GRID_SPAN_X, GRID_SPAN_Y, GRID_SPAN_Z), ((0, 4), (1, 8)), -0.2, 0.2)), 0.5, 2.0)
    walker_speed_vectors = centred(arg_keys[2], (3, NBLK, SLOTS), 1.0, 6.0, ((1, 32),), jnp.float32)
    walker_statistical_mass = jnp.clip(jnp.exp(math.log(2.0) - 1.3862944 * jax.random.uniform(arg_keys[3], (NBLK, SLOTS), jnp.float32) ** block_levels(arg_keys[3], (NBLK, SLOTS), ((0, 32),), -0.2, 0.2)), 0.5, 2.0)
    gaussian_samples = centred(arg_keys[4], (2, 3, NBLK, SLOTS), 1.0, 6.0, ((2, 32),), jnp.float32)
    walker_strip_position = touch_ends(jax.random.randint(arg_keys[5], (NBLK, SLOTS), 0, CZ), jax.random.fold_in(arg_keys[5], 1), 0, CZ - 1).astype(jnp.int32)
    group_active_tally = touch_ends(jax.random.randint(arg_keys[6], (NBLK,), SLOTS // 4, SLOTS + 1), jax.random.fold_in(arg_keys[6], 1), SLOTS // 4, SLOTS).astype(jnp.int32)
    group_resident_strip = touch_ends(jax.random.randint(arg_keys[7], (NBLK,), 0, PENCILS), jax.random.fold_in(arg_keys[7], 1), 0, PENCILS - 1).astype(jnp.int32)
    migrating_group_table = draw_migrating_group_table(jax.random.fold_in(arg_keys[11], 71), 0)
    target_processor_slot_keys = jax.random.split(jax.random.fold_in(arg_keys[9], 1), MIGS // MIG_DEV)
    target_processor_slot_turns = jax.random.permutation(jax.random.fold_in(arg_keys[9], 3), MIGS // MIG_DEV)
    target_processor_slot = jax.vmap(lambda own, number: deal_out(jax.random.fold_in(arg_keys[9], 2), own, number, MIG_DEV, N_YZ, 1, CAP, 2))(target_processor_slot_keys, target_processor_slot_turns).reshape((MIGS, 1))
    entered_strip_slot = touch_ends(jax.random.randint(arg_keys[10], (MIGS,), 0, PENCILS), jax.random.fold_in(arg_keys[10], 1), 0, PENCILS - 1).astype(jnp.int32)
    return dict(flow_speed_field=flow_speed_field, thermal_field=thermal_field, walker_speed_vectors=walker_speed_vectors, walker_statistical_mass=walker_statistical_mass, gaussian_samples=gaussian_samples, walker_strip_position=walker_strip_position, group_active_tally=group_active_tally, group_resident_strip=group_resident_strip, migrating_group_table=migrating_group_table, target_processor_slot=target_processor_slot, entered_strip_slot=entered_strip_slot)


DECAY = 0.6
VISCOSITY = 0.05
COUPLING = 0.02
STRESS_GAIN = 0.005
RELAXATION = 0.5
PAIRS = ((0, 0), (0, 1), (0, 2), (1, 1), (1, 2), (2, 2))
PAIR_INDEX = ((0, 1, 2), (1, 3, 4), (2, 4, 5))

def neighbour(padded, axis, offset):
    sizes = [padded.shape[1] - 2, padded.shape[2] - 2, padded.shape[3] - 2]
    begin = [1, 1, 1]
    begin[axis] = 1 + offset
    return padded[:, begin[0]:begin[0] + sizes[0], begin[1]:begin[1] + sizes[1], begin[2]:begin[2] + sizes[2]]

def laplace(padded):
    total = neighbour(padded, 0, 1) + neighbour(padded, 0, -1)
    total = total + neighbour(padded, 1, 1) + neighbour(padded, 1, -1)
    total = total + neighbour(padded, 2, 1) + neighbour(padded, 2, -1)
    return total - 6.0 * neighbour(padded, 0, 0)

def fluid_step(padded_fields, padded_stress, moments):
    flow = neighbour(padded_fields, 0, 0)[:3]
    heat = neighbour(padded_fields, 0, 0)[3]
    density = moments[0]
    momentum = moments[1:4]
    stress = moments[4:10]
    smooth = laplace(padded_fields)
    slopes = [0.5 * (neighbour(padded_stress, axis, 1) - neighbour(padded_stress, axis, -1)) for axis in range(3)]
    divergence = jnp.stack([slopes[0][PAIR_INDEX[row][0]] + slopes[1][PAIR_INDEX[row][1]] + slopes[2][PAIR_INDEX[row][2]] for row in range(3)])
    new_flow = flow + VISCOSITY * smooth[:3] + COUPLING * (momentum - density[None] * flow) - STRESS_GAIN * divergence
    energy = (stress[0] + stress[3] + stress[5] - 2.0 * lax.optimization_barrier(jnp.sum(momentum * flow, axis=0)) + density * lax.optimization_barrier(jnp.sum(flow * flow, axis=0))) / 3.0
    new_heat = heat + VISCOSITY * smooth[3] + COUPLING * (energy - density * heat)
    return jnp.concatenate([new_flow, new_heat[None]], 0)

def drift_step(start, sampled, noise):
    return sampled[:3] + DECAY * (start - sampled[:3]) + jnp.sqrt((1.0 - DECAY * DECAY) * sampled[3])[None] * noise

def sample(mesh_element_measure, column_x, column_y, cells):
    return jnp.take_along_axis(mesh_element_measure[:, column_x, column_y, :], cells[None], axis=2)

def reference(flow_speed_field, thermal_field, walker_speed_vectors, walker_statistical_mass, gaussian_samples, walker_strip_position, group_active_tally, group_resident_strip, migrating_group_table, target_processor_slot, entered_strip_slot):
    blocks = jnp.arange(NBLK, dtype=jnp.int32)
    device = blocks // BLK_DEV
    home_x = device // N_YZ * CX + group_resident_strip // CY
    home_y = device % N_YZ * CY + group_resident_strip % CY
    mover = jnp.arange(MIGS, dtype=jnp.int32) // MIG_DEV
    moved = mover * BLK_DEV + migrating_group_table
    current_x = home_x.at[moved].set(mover // N_YZ * CX + entered_strip_slot // CY)
    current_y = home_y.at[moved].set(target_processor_slot[:, 0] * CY + entered_strip_slot % CY)
    live = (jnp.arange(SLOTS, dtype=jnp.int32)[None, :] < group_active_tally[:, None]).astype(jnp.float32)
    mesh_element_measure = jnp.concatenate([flow_speed_field, thermal_field[None]], 0)
    first = drift_step(walker_speed_vectors, sample(mesh_element_measure, home_x, home_y, walker_strip_position), gaussian_samples[0])
    second = drift_step(first, sample(mesh_element_measure, current_x, current_y, walker_strip_position), gaussian_samples[1])
    weight = walker_statistical_mass * live
    flat = ((current_x[:, None] * GRID_SPAN_Y + current_y[:, None]) * GRID_SPAN_Z + walker_strip_position).reshape(-1)
    terms = [weight] + [weight * second[row] for row in range(3)] + [weight * second[one] * second[two] for one, two in PAIRS]
    moments = jnp.stack([jax.ops.segment_sum(term.reshape(-1), flat, num_segments=GRID_SPAN_X * GRID_SPAN_Y * GRID_SPAN_Z) for term in terms]).reshape(10, GRID_SPAN_X, GRID_SPAN_Y, GRID_SPAN_Z)
    widths = ((0, 0), (1, 1), (1, 1), (1, 1))
    new_cube = fluid_step(jnp.pad(mesh_element_measure, widths), jnp.pad(moments[4:10], widths), moments)
    after = sample(new_cube, current_x, current_y, walker_strip_position)
    final = second + RELAXATION * (after[:3] - second)
    return (new_cube, final * live[None])
```

```python
import functools
import math

import jax
import jax.numpy as jnp
from jax import lax
from jax.experimental import pallas as pl
from jax.experimental.pallas import tpu as pltpu
from jax.sharding import PartitionSpec as P

DECAY = 0.6
VISCOSITY = 0.05
COUPLING = 0.02
STRESS_GAIN = 0.005
RELAXATION = 0.5
PAIRS = ((0, 0), (0, 1), (0, 2), (1, 1), (1, 2), (2, 2))
PAIR_INDEX = ((0, 1, 2), (1, 3, 4), (2, 4, 5))
MOMENTS = 10
PITCH = 24
SENT = 8
UNROLL = 16
LOAD_ORDER = (8, 9, 10, 7, 6, 0, 1, 5, 3, 4, 2)
X_FACE = tuple(row[0] for row in PAIR_INDEX)
Y_FACE = tuple(row[1] for row in PAIR_INDEX)
MESH = pl.DeviceIdType.MESH
BF16 = jnp.bfloat16
F32 = jnp.float32


def split(x):
    high = x.astype(BF16)
    return high, (x - high.astype(F32)).astype(BF16)


def dot(a, b):
    return jnp.dot(a, b, preferred_element_type=F32)


def dot_last(a, b):
    return lax.dot_general(a, b, (((1,), (1,)), ((), ())), preferred_element_type=F32)


def twice(x, axis):
    return jnp.concatenate([x, x], axis=axis)


def pick(onehot_twice, x):
    return dot(onehot_twice, jnp.concatenate(split(x), axis=0))


def lanes(x, index):
    return jnp.take_along_axis(x, index, axis=1, mode="promise_in_bounds")


def onehot(condition):
    return jnp.where(condition, 1.0, 0.0)


def drift(start, u, spread, noise):
    return u + DECAY * (start - u) + spread * noise


def deposit(count, v_ref, cells_ref, pb_ref):
    width = v_ref.shape[1]
    slots = cells_ref.shape[1]
    half = count // 2
    unroll = math.gcd(half, UNROLL)
    where = lax.broadcasted_iota(jnp.int32, (width, slots), 0)
    none = jnp.zeros((8, slots), F32)
    mine = lax.broadcasted_iota(jnp.int32, (8, slots), 0) < MOMENTS - 8

    def some(step, carry):
        for t in range(unroll):
            n = step * unroll + t
            start = pl.multiple_of(n * 2 * PITCH, 2 * PITCH)
            rows = [v_ref[pl.ds(start + 8 * part, 8), :] for part in range(6)]
            left = [rows[0], jnp.where(mine, rows[1], 0.0), none, rows[3], jnp.where(mine, rows[4], 0.0), none]
            right = [none, jnp.where(mine, 0.0, rows[1]), rows[2], none, jnp.where(mine, 0.0, rows[4]), rows[5]]
            lhs = jnp.concatenate(
                [jnp.concatenate(side, axis=0).astype(BF16) for side in (left, right)], axis=1
            )
            hot = jnp.concatenate(
                [onehot(cells_ref[pl.ds(n + block, 1), :] == where).astype(BF16) for block in (0, half)], axis=1
            )
            out = dot_last(lhs, hot)
            pb_ref[pl.ds(pl.multiple_of(n * PITCH, 8), PITCH), :] = out[:PITCH] + out[PITCH:]
        return carry

    lax.fori_loop(0, half // unroll, some, 0)


def put_terms(v_ref, count, weight, second):
    half = count // 2
    weighted = [weight * second[row] for row in range(3)]
    terms = [weight] + weighted + [weighted[one] * second[two] for one, two in PAIRS]
    for k, term in enumerate(terms):
        high = term.astype(BF16).astype(F32)
        for part, value in enumerate((high, term - high)):
            for block in range(2):
                v_ref[pl.ds(part * PITCH + block * MOMENTS + k, half, stride=2 * PITCH), :] = value[
                    block * half : (block + 1) * half
                ]


def deposited(pb_ref, count, k):
    half = count // 2
    return jnp.concatenate(
        [pb_ref[pl.ds(block * MOMENTS + k, half, stride=PITCH), :] for block in range(2)], axis=0
    )


def kernel(
    n,
    n_gx,
    spans,
    *refs,
):
    sources, (fields_out, speed_out), held, load_s = refs[:11], refs[11:13], refs[13:24], refs[24]
    flow, heat, speed, mass, noise, cells, tally, home, table, target, entered = held
    (
    v_ref,
    pb_ref,
    second_ref,
    cells_a,
    moments,
    wide,
    face_send,
    face_recv,
    stress_send,
    stress_recv,
    out_ref,
    in_ref,
    back_send,
    back_recv,
    out_s,
    out_r,
    face_s,
    face_r,
    stress_s,
    stress_r,
    back_s,
    back_r,
    ) = refs[25:]
    loads = [
        pltpu.make_async_copy(source, kept, load_s.at[i])
        for i, (source, kept) in enumerate(zip(sources, held))
    ]
    X, Y, Z = spans
    pencils = X * Y
    blocks, slots = mass.shape
    moving = table.shape[1]
    cap = 2 * moving // n
    received = n * cap
    rows = out_ref.shape[0] // n
    back_rows = back_send.shape[0] // n
    gx = lax.axis_index("gx")
    me = lax.axis_index("yz")
    order = sorted(range(1, n), key=lambda i: abs(2 * i - n))
    peers = [(i, lax.rem(me + i, n), lax.rem(me + n - i, n)) for i in order]
    for i in LOAD_ORDER:
        loads[i].start()

    barrier = pltpu.get_barrier_semaphore()
    for _, peer, _ in peers:
        pl.semaphore_signal(barrier, inc=1, device_id={"yz": peer}, device_id_type=MESH)

    @pl.when(gx > 0)
    def _():
        pl.semaphore_signal(barrier, inc=1, device_id={"gx": gx - 1}, device_id_type=MESH)

    @pl.when(gx < n_gx - 1)
    def _():
        pl.semaphore_signal(barrier, inc=1, device_id={"gx": gx + 1}, device_id_type=MESH)

    sides = (
        (0, 1, gx > 0, gx == 0, {"gx": gx - 1}),
        (1, 0, gx < n_gx - 1, gx == n_gx - 1, {"gx": gx + 1}),
        (2, 3, me > 0, me == 0, {"yz": me - 1}),
        (3, 2, me < n - 1, me == n - 1, {"yz": me + 1}),
    )
    for side, _, _, edge, _ in sides:

        @pl.when(edge)
        def _(side=side):
            face_recv[side] = jnp.zeros(face_recv.shape[1:], F32)
            stress_recv[side] = jnp.zeros(stress_recv.shape[1:], F32)

    def face_copy(side, other, where, send, recv, send_sem, recv_sem):
        return pltpu.make_async_remote_copy(
            src_ref=send.at[side],
            dst_ref=recv.at[other],
            send_sem=send_sem.at[side],
            recv_sem=recv_sem.at[other],
            device_id=where,
            device_id_type=MESH,
        )

    def faces_start(send, recv, send_sem, recv_sem):
        for side, other, there, _, where in sides:

            @pl.when(there)
            def _(side=side, other=other, where=where):
                face_copy(side, other, where, send, recv, send_sem, recv_sem).start()

    def faces_wait(send, recv, send_sem, recv_sem):
        for side, _, there, _, where in sides:

            @pl.when(there)
            def _(side=side, where=where):
                face_copy(side, side, where, send, recv, send_sem, recv_sem).wait_recv()

    def faces_sent(send, recv, send_sem, recv_sem):
        for side, other, there, _, where in sides:

            @pl.when(there)
            def _(side=side, other=other, where=where):
                face_copy(side, other, where, send, recv, send_sem, recv_sem).wait_send()

    face_args = (face_send, face_recv, face_s, face_r)
    stress_args = (stress_send, stress_recv, stress_s, stress_r)

    def all_copy(i, peer, send, recv, height, pitch, send_sem, recv_sem):
        return pltpu.make_async_remote_copy(
            src_ref=send.at[pl.ds(pl.multiple_of(peer * pitch, 8), height), :],
            dst_ref=recv.at[pl.ds(pl.multiple_of(me * pitch, 8), height), :],
            send_sem=send_sem.at[i],
            recv_sem=recv_sem.at[i],
            device_id={"yz": peer},
            device_id_type=MESH,
        )

    def all_start(send, recv, height, pitch, send_sem, recv_sem):
        for i, peer, _ in peers:
            all_copy(i, peer, send, recv, height, pitch, send_sem, recv_sem).start()

    def all_wait(send, recv, height, pitch, send_sem, recv_sem):
        for i, _, source in peers:
            pltpu.make_async_remote_copy(
                src_ref=send.at[pl.ds(pl.multiple_of(source * pitch, 8), height), :],
                dst_ref=recv.at[pl.ds(pl.multiple_of(source * pitch, 8), height), :],
                send_sem=send_sem.at[i],
                recv_sem=recv_sem.at[i],
                device_id={"yz": source},
                device_id_type=MESH,
            ).wait_recv()

    def all_sent(send, recv, height, pitch, send_sem, recv_sem):
        for i, peer, _ in peers:
            all_copy(i, peer, send, recv, height, pitch, send_sem, recv_sem).wait_send()

    pay_args = (out_ref, in_ref, SENT * cap + 1, rows, out_s, out_r)
    back_args = (back_send, back_recv, 3 * cap, back_rows, back_s, back_r)

    def landed(*which):
        for i in which:
            loads[i].wait()

    landed(8, 9, 10, 7, 6)
    iota = functools.partial(lax.broadcasted_iota, jnp.int32)

    def folded(shape, axis, period):
        place = iota(shape, axis)
        return jnp.where(place < period, place, place - period)

    eye = iota((moving, moving), 0) == iota((moving, moving), 1)
    target_row = target[...]
    target_col = jnp.sum(jnp.where(eye, target_row, 0), axis=1, keepdims=True)
    earlier = (target_col == target_row) & (iota((moving, moving), 0) < iota((moving, moving), 1))
    rank = jnp.sum(jnp.where(earlier, 1, 0), axis=0, keepdims=True)
    slot_row = rank * n + target_row
    slot_hot = onehot(folded((2 * received, moving), 0, received) == slot_row)
    block_hot = onehot(iota((blocks, moving), 0) == table[...]).astype(BF16)
    from_block = dot_last(slot_hot[:received].astype(BF16), block_hot).astype(BF16)
    from_twice = twice(from_block, 1)
    to_block = dot_last(block_hot, slot_hot.astype(BF16))
    moved = jnp.sum(to_block, axis=1, keepdims=True) > 0.5
    to_block = to_block.astype(BF16)
    pencil_out = jnp.sum(slot_hot[:received] * entered[...].astype(F32), axis=1, keepdims=True)

    home_t = onehot(folded((2 * pencils, blocks), 0, pencils) == home[...])
    home_hot = home_t.T.astype(BF16)
    home_t = twice(home_t[:pencils].astype(BF16), 1)
    live = onehot(iota((slots, blocks), 0) < tally[...]).T

    landed(0, 1)
    u = [pick(home_hot, flow[c]) for c in range(3)]
    temp = pick(home_hot, heat[...])
    for c in range(4):
        grid = flow.at[c] if c < 3 else heat
        face_send[0, c] = grid[pl.ds(0, Y), :]
        face_send[1, c] = grid[pl.ds((X - 1) * Y, Y), :]
        face_send[2, c] = grid[pl.ds(0, X, stride=Y), :]
        face_send[3, c] = grid[pl.ds(Y - 1, X, stride=Y), :]

    landed(5, 3)
    where = cells[...]
    u = [lanes(u[c], where) for c in range(3)]
    spread = jnp.sqrt((1.0 - DECAY * DECAY) * lanes(temp, where))
    weight = mass[...] * live

    def send_row(c, value):
        for j in range(cap):
            out_ref[pl.ds(c * cap + j, n, stride=rows), :] = value[j * n : (j + 1) * n]

    send_row(6, pick(from_twice, weight))
    send_row(7, dot(from_block, where.astype(F32).astype(BF16)))
    group = lax.div(iota((n, slots), 1), slots // cap)
    pencil_row = jnp.broadcast_to(pencil_out[:n], (n, slots))
    for j in range(1, cap):
        pencil_row = jnp.where(group == j, pencil_out[j * n : (j + 1) * n], pencil_row)
    out_ref[pl.ds(SENT * cap, n, stride=rows), :] = pencil_row

    landed(4)
    for c in range(3):
        send_row(3 + c, pick(from_twice, noise[3 + c]))

    landed(2)
    first = [drift(speed[c], u[c], spread, noise[c]) for c in range(3)]
    for c in range(3):
        send_row(c, pick(from_twice, first[c]))

    expected = n - 1 + jnp.where(gx > 0, 1, 0) + jnp.where(gx < n_gx - 1, 1, 0)
    pl.semaphore_wait(barrier, expected)
    all_start(*pay_args)
    faces_start(*face_args)
    own = pl.ds(pl.multiple_of(me * rows, 8), rows)
    in_ref[own, :] = out_ref[own, :]

    second = [drift(first[c], u[c], spread, noise[3 + c]) for c in range(3)]
    for c in range(3):
        second_ref[c] = second[c]
    put_terms(v_ref, blocks, jnp.where(moved, 0.0, weight), second)
    deposit(blocks, v_ref, cells, pb_ref)
    for k in range(MOMENTS):
        moments[k] = pick(home_t, deposited(pb_ref, blocks, k))

    all_wait(*pay_args)
    got = [
        jnp.concatenate(
            [in_ref[pl.ds(c * cap + j, n, stride=rows), :] for j in range(cap)], axis=0
        )
        for c in range(SENT)
    ]
    where_a = got[7].astype(jnp.int32)
    cells_a[...] = where_a
    pencil_row = in_ref[pl.ds(SENT * cap, n, stride=rows), :]
    pencil_in = jnp.concatenate(
        [lanes(pencil_row, jnp.full((n, slots), j * (slots // cap), jnp.int32)) for j in range(cap)], axis=0
    ).astype(jnp.int32)
    pencil_hot = onehot(pencil_in[:, : 2 * pencils] == folded((received, 2 * pencils), 1, pencils))
    pencil_t = twice(pencil_hot[:, :pencils], 0).T.astype(BF16)
    pencil_hot = pencil_hot.astype(BF16)
    u_a = [lanes(pick(pencil_hot, flow[c]), where_a) for c in range(3)]
    temp_a = lanes(pick(pencil_hot, heat[...]), where_a)
    spread_a = jnp.sqrt((1.0 - DECAY * DECAY) * temp_a)
    second_a = [drift(got[c], u_a[c], spread_a, got[3 + c]) for c in range(3)]
    put_terms(v_ref, received, got[6], second_a)
    deposit(received, v_ref, cells_a, pb_ref)

    def total(k):
        moments[k] = moments[k] + pick(pencil_t, deposited(pb_ref, received, k))

    for k in range(4, MOMENTS):
        total(k)
    for row in range(3):
        k = 4 + X_FACE[row]
        stress_send[0, row] = moments[k, pl.ds(0, Y), :]
        stress_send[1, row] = moments[k, pl.ds(pencils - Y, Y), :]
        k = 4 + Y_FACE[row]
        stress_send[2, row] = moments[k, pl.ds(0, X, stride=Y), :]
        stress_send[3, row] = moments[k, pl.ds(Y - 1, X, stride=Y), :]
    faces_start(*stress_args)
    for k in range(4):
        total(k)

    lane = iota((pencils, Z), 1)

    def along_z(x, step):
        if step > 0:
            return jnp.where(lane == Z - 1, 0.0, pltpu.roll(x, Z - 1, 1))
        return jnp.where(lane == 0, 0.0, pltpu.roll(x, 1, 1))

    def fill(slot, value):
        wide[slot, 1 : X + 1, 8 : 8 + Y, :] = value.reshape(X, Y, Z)

    def edge_x(slot, halo, c):
        wide[slot, 0, 8 : 8 + Y, :] = halo[0, c]
        wide[slot, X + 1, 8 : 8 + Y, :] = halo[1, c]

    def edge_y(slot, halo, c):
        for x in range(X):
            wide[slot, x + 1, 7:8, :] = halo[2, c, x : x + 1]
            wide[slot, x + 1, 8 + Y : 9 + Y, :] = halo[3, c, x : x + 1]

    def along_x(slot, step):
        return wide[slot, 1 + step : 1 + step + X, 8 : 8 + Y, :].reshape(pencils, Z)

    def along_y(slot, step):
        return wide[slot, 1 : X + 1, 8 + step : 8 + step + Y, :].reshape(pencils, Z)

    faces_wait(*face_args)
    f = [flow[0], flow[1], flow[2], heat[...]]
    base = []
    for c in range(4):
        fill(c, f[c])
        edge_x(c, face_recv, c)
        edge_y(c, face_recv, c)
        smooth = along_x(c, 1) + along_x(c, -1) + along_y(c, 1) + along_y(c, -1)
        smooth = smooth + along_z(f[c], 1) + along_z(f[c], -1) - 6.0 * f[c]
        base.append(f[c] + VISCOSITY * smooth)
    density = moments[0]
    momentum = [moments[1 + c] for c in range(3)]
    for c in range(3):
        base[c] = base[c] + COUPLING * (momentum[c] - density * f[c])
    dots = momentum[0] * f[0] + momentum[1] * f[1] + momentum[2] * f[2]
    squares = f[0] * f[0] + f[1] * f[1] + f[2] * f[2]
    energy = (moments[4] + moments[7] + moments[9] - 2.0 * dots + density * squares) / 3.0
    fields_out[3] = base[3] + COUPLING * (energy - density * f[3])
    stress = [moments[4 + s] for s in range(6)]
    for s in range(5):
        fill(4 + s, stress[s])
    for row in range(3):
        sz = stress[PAIR_INDEX[row][2]]
        base[row] = base[row] - (0.5 * STRESS_GAIN) * (along_z(sz, 1) - along_z(sz, -1))

    faces_wait(*stress_args)
    for row in range(3):
        edge_x(4 + X_FACE[row], stress_recv, row)
        edge_y(4 + Y_FACE[row], stress_recv, row)
    fresh = []
    for row in range(3):
        sx, sy = 4 + X_FACE[row], 4 + Y_FACE[row]
        slope = along_x(sx, 1) - along_x(sx, -1) + along_y(sy, 1) - along_y(sy, -1)
        value = base[row] - (0.5 * STRESS_GAIN) * slope
        fields_out[row] = value
        fresh.append(jnp.concatenate(split(value), axis=0))

    for c in range(3):
        w = lanes(dot(pencil_hot, fresh[c]), where_a)
        third = second_a[c] + RELAXATION * (w - second_a[c])
        for j in range(cap):
            back_send[pl.ds(c * cap + j, n, stride=back_rows), :] = third[j * n : (j + 1) * n]
    all_start(*back_args)
    own = pl.ds(pl.multiple_of(me * back_rows, 8), back_rows)
    back_recv[own, :] = back_send[own, :]
    for c in range(3):
        w = lanes(dot(home_hot, fresh[c]), where)
        now = second_ref[c]
        second_ref[c] = live * (now + RELAXATION * (w - now))
    all_wait(*back_args)
    for c in range(3):
        returned = jnp.concatenate(
            [back_recv[pl.ds(c * cap + j, n, stride=back_rows), :] for j in range(cap)], axis=0
        )
        speed_out[c] = jnp.where(moved, live * pick(to_block, returned), second_ref[c])

    all_sent(*pay_args)
    faces_sent(*face_args)
    faces_sent(*stress_args)
    all_sent(*back_args)


def put_out(fields, velocity, fields_out, velocity_out, sems):
    copies = (
        pltpu.make_async_copy(fields, fields_out, sems.at[0]),
        pltpu.make_async_copy(velocity, velocity_out, sems.at[1]),
    )
    for copy in copies:
        copy.start()
    for copy in copies:
        copy.wait()


def shards(
    flow_speed_field,
    thermal_field,
    walker_speed_vectors,
    walker_statistical_mass,
    gaussian_samples,
    walker_strip_position,
    group_active_tally,
    group_resident_strip,
    migrating_group_table,
    target_processor_slot,
    entered_strip_slot,
):
    n = lax.axis_size("yz")
    n_gx = lax.axis_size("gx")
    X, Y, Z = thermal_field.shape
    blocks, slots = walker_statistical_mass.shape
    moving = migrating_group_table.shape[0]
    cap = 2 * moving // n
    received = n * cap
    rows = -(-(SENT * cap + 1) // 8) * 8
    back_rows = -(-3 * cap // 8) * 8
    operands = (
        flow_speed_field.reshape(3, X * Y, Z),
        thermal_field.reshape(X * Y, Z),
        walker_speed_vectors,
        walker_statistical_mass,
        gaussian_samples.reshape(6, blocks, slots),
        walker_strip_position,
        group_active_tally.reshape(1, blocks),
        group_resident_strip.reshape(1, blocks),
        migrating_group_table.reshape(1, moving),
        target_processor_slot.reshape(1, moving),
        entered_strip_slot.reshape(1, moving),
    )
    vmem = pl.BlockSpec(memory_space=pltpu.VMEM)
    fields, velocity = pl.pallas_call(
        functools.partial(kernel, n, n_gx, (X, Y, Z)),
        out_shape=(
            pltpu.VMEM((4, X * Y, Z), F32),
            pltpu.VMEM((3, blocks, slots), F32),
        ),
        in_specs=[pl.BlockSpec(memory_space=pltpu.HBM)] * 11,
        out_specs=(vmem, vmem),
        scratch_shapes=[pltpu.VMEM(x.shape, x.dtype) for x in operands]
        + [pltpu.SemaphoreType.DMA((11,))]
        + [
            pltpu.VMEM((max(blocks, received) * PITCH, slots), F32),
            pltpu.VMEM((max(blocks, received) // 2 * PITCH, Z), F32),
            pltpu.VMEM((3, blocks, slots), F32),
            pltpu.VMEM((received, slots), jnp.int32),
            pltpu.VMEM((MOMENTS, X * Y, Z), F32),
            pltpu.VMEM((9, X + 2, 24, Z), F32),
            pltpu.VMEM((4, 4, 8, Z), F32),
            pltpu.VMEM((4, 4, 8, Z), F32),
            pltpu.VMEM((4, 3, 8, Z), F32),
            pltpu.VMEM((4, 3, 8, Z), F32),
            pltpu.VMEM((n * rows, slots), F32),
            pltpu.VMEM((n * rows, slots), F32),
            pltpu.VMEM((n * back_rows, slots), F32),
            pltpu.VMEM((n * back_rows, slots), F32),
            pltpu.SemaphoreType.DMA((n,)),
            pltpu.SemaphoreType.DMA((n,)),
            pltpu.SemaphoreType.DMA((4,)),
            pltpu.SemaphoreType.DMA((4,)),
            pltpu.SemaphoreType.DMA((4,)),
            pltpu.SemaphoreType.DMA((4,)),
            pltpu.SemaphoreType.DMA((n,)),
            pltpu.SemaphoreType.DMA((n,)),
        ],
        compiler_params=pltpu.CompilerParams(
            collective_id=0, has_side_effects=True, vmem_limit_bytes=32 * 1024 * 1024
        ),
    )(*(pltpu.with_memory_space_constraint(x, pltpu.HBM) for x in operands))
    hbm = pl.BlockSpec(memory_space=pltpu.HBM)
    fields, velocity = pl.pallas_call(
        put_out,
        out_shape=(
            jax.ShapeDtypeStruct((4, X * Y, Z), F32),
            jax.ShapeDtypeStruct((3, blocks, slots), F32),
        ),
        in_specs=[vmem, vmem],
        out_specs=(hbm, hbm),
        scratch_shapes=[pltpu.SemaphoreType.DMA((2,))],
        compiler_params=pltpu.CompilerParams(vmem_limit_bytes=32 * 1024 * 1024),
    )(fields, velocity)
    return fields.reshape(4, X, Y, Z), velocity


def solution(mesh):
    return jax.shard_map(
        shards,
        mesh=mesh,
        in_specs=(
            P(None, "gx", "yz", None),
            P("gx", "yz", None),
            P(None, ("gx", "yz"), None),
            P(("gx", "yz"), None),
            P(None, None, ("gx", "yz"), None),
            P(("gx", "yz"), None),
            P(("gx", "yz")),
            P(("gx", "yz")),
            P(("gx", "yz")),
            P(("gx", "yz"), None),
            P(("gx", "yz")),
        ),
        out_specs=(P(None, "gx", "yz", None), P(None, ("gx", "yz"), None)),
        check_vma=False,
    )
```

```python
import functools
import math

import jax
import jax.numpy as jnp
from jax import lax
from jax.experimental import pallas as pl
from jax.experimental.pallas import tpu as pltpu
from jax.sharding import PartitionSpec as P

DECAY = 0.6
VISCOSITY = 0.05
COUPLING = 0.02
STRESS_GAIN = 0.005
RELAXATION = 0.5
PAIRS = ((0, 0), (0, 1), (0, 2), (1, 1), (1, 2), (2, 2))
PAIR_INDEX = ((0, 1, 2), (1, 3, 4), (2, 4, 5))
MOMENTS = 10
PITCH = 24
SENT = 8
UNROLL = 16
LOAD_ORDER = (8, 9, 10, 7, 6, 0, 1, 5, 3, 4, 2)
X_FACE = tuple(row[0] for row in PAIR_INDEX)
Y_FACE = tuple(row[1] for row in PAIR_INDEX)
MESH = pl.DeviceIdType.MESH
BF16 = jnp.bfloat16
F32 = jnp.float32


def split(x):
    high = x.astype(BF16)
    return high, (x - high.astype(F32)).astype(BF16)


def dot(a, b):
    return jnp.dot(a, b, preferred_element_type=F32)


def dot_last(a, b):
    return lax.dot_general(a, b, (((1,), (1,)), ((), ())), preferred_element_type=F32)


def twice(x, axis):
    return jnp.concatenate([x, x], axis=axis)


def pick(onehot_twice, x):
    return dot(onehot_twice, jnp.concatenate(split(x), axis=0))


def lanes(x, index):
    return jnp.take_along_axis(x, index, axis=1, mode="promise_in_bounds")


def onehot(condition):
    return jnp.where(condition, 1.0, 0.0)


def partner(me, i, n):
    peer, bit = 0, 1
    while bit < n:
        own = lax.rem(lax.div(me, bit), 2)
        peer = peer + bit * (1 - own if i & bit else own)
        bit *= 2
    return peer


def drift(start, u, spread, noise):
    return u + DECAY * (start - u) + spread * noise


def deposit(count, v_ref, cells_ref, pb_ref, first=0, last=None):
    width = v_ref.shape[1]
    slots = cells_ref.shape[1]
    half = count // 2
    unroll = math.gcd(half, UNROLL)
    where = lax.broadcasted_iota(jnp.int32, (width, slots), 0)
    none = jnp.zeros((8, slots), F32)
    mine = lax.broadcasted_iota(jnp.int32, (8, slots), 0) < MOMENTS - 8

    def some(step, carry):
        for t in range(unroll):
            n = step * unroll + t
            start = pl.multiple_of(n * 2 * PITCH, 2 * PITCH)
            rows = [v_ref[pl.ds(start + 8 * part, 8), :] for part in range(6)]
            left = [rows[0], jnp.where(mine, rows[1], 0.0), none, rows[3], jnp.where(mine, rows[4], 0.0), none]
            right = [none, jnp.where(mine, 0.0, rows[1]), rows[2], none, jnp.where(mine, 0.0, rows[4]), rows[5]]
            lhs = jnp.concatenate(
                [jnp.concatenate(side, axis=0).astype(BF16) for side in (left, right)], axis=1
            )
            hot = jnp.concatenate(
                [onehot(cells_ref[pl.ds(n + block, 1), :] == where).astype(BF16) for block in (0, half)], axis=1
            )
            out = dot_last(lhs, hot)
            pb_ref[pl.ds(pl.multiple_of(n * PITCH, 8), PITCH), :] = out[:PITCH] + out[PITCH:]
        return carry

    lax.fori_loop(first, half // unroll if last is None else last, some, 0)


def put_terms(v_ref, count, weight, second):
    half = count // 2
    weighted = [weight * second[row] for row in range(3)]
    terms = [weight] + weighted + [weighted[one] * second[two] for one, two in PAIRS]
    for k, term in enumerate(terms):
        high = term.astype(BF16).astype(F32)
        for part, value in enumerate((high, term - high)):
            for block in range(2):
                v_ref[pl.ds(part * PITCH + block * MOMENTS + k, half, stride=2 * PITCH), :] = value[
                    block * half : (block + 1) * half
                ]


def deposited(pb_ref, count, k):
    half = count // 2
    return jnp.concatenate(
        [pb_ref[pl.ds(block * MOMENTS + k, half, stride=PITCH), :] for block in range(2)], axis=0
    )


def kernel(
    n,
    n_gx,
    spans,
    *refs,
):
    sources, (fields_out, speed_out), held, load_s = refs[:11], refs[11:13], refs[13:24], refs[24]
    flow, heat, speed, mass, noise, cells, tally, home, table, target, entered = held
    (
    v_ref,
    pb_ref,
    second_ref,
    cells_a,
    moments,
    wide,
    face_send,
    face_recv,
    stress_send,
    stress_recv,
    out_ref,
    in_ref,
    back_send,
    back_recv,
    out_s,
    out_r,
    face_s,
    face_r,
    stress_s,
    stress_r,
    back_s,
    back_r,
    ) = refs[25:]
    loads = [
        pltpu.make_async_copy(source, kept, load_s.at[i])
        for i, (source, kept) in enumerate(zip(sources, held))
    ]
    X, Y, Z = spans
    pencils = X * Y
    blocks, slots = mass.shape
    moving = table.shape[1]
    cap = 2 * moving // n
    received = n * cap
    rows = out_ref.shape[0] // n
    back_rows = back_send.shape[0] // n
    gx = lax.axis_index("gx")
    me = lax.axis_index("yz")
    far = [partner(me, i, n) for i in range(n - 1, n // 2 - 1, -1)]
    near = [partner(me, i, n) for i in range(n // 2 - 1, 0, -1)]
    odd = lax.rem(gx, 2)
    turns = [j + odd * (n - 2 - 2 * j) for j in range(n - 1)]
    others = [j + lax.div(j + n - me, n) for j in turns]
    group = received // 2
    base_a = n // 2 * jnp.minimum(lax.div(me, n // 4), 1)
    base_b = n // 2 - base_a
    barrier = pltpu.get_barrier_semaphore()
    for peer in far + near:
        pl.semaphore_signal(barrier, inc=1, device_id={"yz": peer}, device_id_type=MESH)

    @pl.when(gx > 0)
    def _():
        pl.semaphore_signal(barrier, inc=1, device_id={"gx": gx - 1}, device_id_type=MESH)

    @pl.when(gx < n_gx - 1)
    def _():
        pl.semaphore_signal(barrier, inc=1, device_id={"gx": gx + 1}, device_id_type=MESH)

    for i in LOAD_ORDER:
        loads[i].start()

    sides = (
        (0, 1, gx > 0, gx == 0, {"gx": gx - 1}),
        (1, 0, gx < n_gx - 1, gx == n_gx - 1, {"gx": gx + 1}),
        (2, 3, me > 0, me == 0, {"yz": me - 1}),
        (3, 2, me < n - 1, me == n - 1, {"yz": me + 1}),
    )
    for side, _, _, edge, _ in sides:

        @pl.when(edge)
        def _(side=side):
            face_recv[side] = jnp.zeros(face_recv.shape[1:], F32)
            stress_recv[side] = jnp.zeros(stress_recv.shape[1:], F32)

    def face_copy(side, other, where, send, recv, send_sem, recv_sem):
        return pltpu.make_async_remote_copy(
            src_ref=send.at[side],
            dst_ref=recv.at[other],
            send_sem=send_sem.at[side],
            recv_sem=recv_sem.at[other],
            device_id=where,
            device_id_type=MESH,
        )

    def faces_start(send, recv, send_sem, recv_sem):
        for side, other, there, _, where in sides:

            @pl.when(there)
            def _(side=side, other=other, where=where):
                face_copy(side, other, where, send, recv, send_sem, recv_sem).start()

    def faces_wait(send, recv, send_sem, recv_sem):
        for side, _, there, _, where in sides:

            @pl.when(there)
            def _(side=side, where=where):
                face_copy(side, side, where, send, recv, send_sem, recv_sem).wait_recv()

    def faces_sent(send, recv, send_sem, recv_sem):
        for side, other, there, _, where in sides:

            @pl.when(there)
            def _(side=side, other=other, where=where):
                face_copy(side, other, where, send, recv, send_sem, recv_sem).wait_send()

    face_args = (face_send, face_recv, face_s, face_r)
    stress_args = (stress_send, stress_recv, stress_s, stress_r)

    def all_copy(peer, source, send, recv, height, pitch, send_sem, recv_sem):
        return pltpu.make_async_remote_copy(
            src_ref=send.at[pl.ds(pl.multiple_of(peer * pitch, 8), height), :],
            dst_ref=recv.at[pl.ds(pl.multiple_of(source * pitch, 8), height), :],
            send_sem=send_sem.at[peer],
            recv_sem=recv_sem.at[source],
            device_id={"yz": peer},
            device_id_type=MESH,
        )

    def all_start(peers, *args):
        for peer in peers:
            all_copy(peer, me, *args).start()

    def all_wait(peers, *args):
        for peer in peers:
            all_copy(peer, peer, *args).wait_recv()

    def half_wait(base, *args):
        for j in range(n // 2):
            @pl.when(base + j != me)
            def _(j=j):
                all_copy(base + j, base + j, *args).wait_recv()

    def all_sent(peers, *args):
        for peer in peers:
            all_copy(peer, me, *args).wait_send()

    pay_args = (out_ref, in_ref, SENT * cap + 1, rows, out_s, out_r)
    back_args = (back_send, back_recv, 3 * cap, back_rows, back_s, back_r)

    def landed(*which):
        for i in which:
            loads[i].wait()

    landed(8, 9, 10, 7, 6)
    iota = functools.partial(lax.broadcasted_iota, jnp.int32)

    def folded(shape, axis, period):
        place = iota(shape, axis)
        return jnp.where(place < period, place, place - period)

    eye = iota((moving, moving), 0) == iota((moving, moving), 1)
    target_row = target[...]
    target_col = jnp.sum(jnp.where(eye, target_row, 0), axis=1, keepdims=True)
    earlier = (target_col == target_row) & (iota((moving, moving), 0) < iota((moving, moving), 1))
    rank = jnp.sum(jnp.where(earlier, 1, 0), axis=0, keepdims=True)
    slot_row = rank * n + target_row
    slot_hot = onehot(folded((2 * received, moving), 0, received) == slot_row)
    block_hot = onehot(iota((blocks, moving), 0) == table[...]).astype(BF16)
    from_block = dot_last(slot_hot[:received].astype(BF16), block_hot).astype(BF16)
    from_twice = twice(from_block, 1)
    to_block = dot_last(block_hot, slot_hot.astype(BF16))
    moved = jnp.sum(to_block, axis=1, keepdims=True) > 0.5
    to_block = to_block.astype(BF16)
    pencil_out = jnp.sum(slot_hot[:received] * entered[...].astype(F32), axis=1, keepdims=True)

    home_t = onehot(folded((2 * pencils, blocks), 0, pencils) == home[...])
    home_hot = home_t.T.astype(BF16)
    home_t = twice(home_t[:pencils].astype(BF16), 1)
    live = onehot(iota((slots, blocks), 0) < tally[...]).T

    landed(0, 1)
    u = [pick(home_hot, flow[c]) for c in range(3)]
    temp = pick(home_hot, heat[...])
    for c in range(4):
        grid = flow.at[c] if c < 3 else heat
        face_send[0, c] = grid[pl.ds(0, Y), :]
        face_send[1, c] = grid[pl.ds((X - 1) * Y, Y), :]
        face_send[2, c] = grid[pl.ds(0, X, stride=Y), :]
        face_send[3, c] = grid[pl.ds(Y - 1, X, stride=Y), :]

    landed(5, 3)
    where = cells[...]
    u = [lanes(u[c], where) for c in range(3)]
    spread = jnp.sqrt((1.0 - DECAY * DECAY) * lanes(temp, where))
    weight = mass[...] * live

    def send_row(c, value):
        for j in range(cap):
            out_ref[pl.ds(c * cap + j, n, stride=rows), :] = value[j * n : (j + 1) * n]

    send_row(6, pick(from_twice, weight))
    send_row(7, dot(from_block, where.astype(F32).astype(BF16)))
    place = lax.div(iota((n, slots), 1), slots // cap)
    pencil_row = jnp.broadcast_to(pencil_out[:n], (n, slots))
    for j in range(1, cap):
        pencil_row = jnp.where(place == j, pencil_out[j * n : (j + 1) * n], pencil_row)
    out_ref[pl.ds(SENT * cap, n, stride=rows), :] = pencil_row

    landed(4)
    for c in range(3):
        send_row(3 + c, pick(from_twice, noise[3 + c]))

    landed(2)
    first = [drift(speed[c], u[c], spread, noise[c]) for c in range(3)]
    for c in range(3):
        send_row(c, pick(from_twice, first[c]))

    expected = n - 1 + jnp.where(gx > 0, 1, 0) + jnp.where(gx < n_gx - 1, 1, 0)
    pl.semaphore_wait(barrier, expected)
    late = lax.rem(gx, 2) == 1

    @pl.when(jnp.logical_not(late))
    def _():
        all_start(far + near, *pay_args)

    faces_start(*face_args)
    own = pl.ds(pl.multiple_of(me * rows, 8), rows)
    in_ref[own, :] = out_ref[own, :]

    second = [drift(first[c], u[c], spread, noise[3 + c]) for c in range(3)]
    for c in range(3):
        second_ref[c] = second[c]
    put_terms(v_ref, blocks, jnp.where(moved, 0.0, weight), second)
    deposit(blocks, v_ref, cells, pb_ref, 0, 3)

    @pl.when(late)
    def _():
        all_start(far + near, *pay_args)

    deposit(blocks, v_ref, cells, pb_ref, 3)
    for k in range(MOMENTS):
        moments[k] = pick(home_t, deposited(pb_ref, blocks, k))

    def migrants(side, base):
        def taken(row):
            return in_ref[pl.ds(base * rows + row, n // 2, stride=rows), :]

        got = [jnp.concatenate([taken(c * cap + j) for j in range(cap)], axis=0) for c in range(SENT)]
        where = got[7].astype(jnp.int32)
        cells_a[side] = where
        pencil_row = taken(SENT * cap)
        pencil = jnp.concatenate(
            [lanes(pencil_row, jnp.full((n // 2, slots), j * (slots // cap), jnp.int32)) for j in range(cap)], axis=0
        ).astype(jnp.int32)
        hot = onehot(pencil[:, : 2 * pencils] == folded((group, 2 * pencils), 1, pencils))
        hot_t = twice(hot[:, :pencils], 0).T.astype(BF16)
        hot = hot.astype(BF16)
        u = [lanes(pick(hot, flow[c]), where) for c in range(3)]
        spread = jnp.sqrt((1.0 - DECAY * DECAY) * lanes(pick(hot, heat[...]), where))
        second = [drift(got[c], u[c], spread, got[3 + c]) for c in range(3)]
        put_terms(v_ref, group, got[6], second)
        deposit(group, v_ref, cells_a.at[side], pb_ref)
        return where, hot, hot_t, second

    def total(hot_t, k):
        moments[k] = moments[k] + pick(hot_t, deposited(pb_ref, group, k))

    half_wait(base_a, *pay_args)
    where_n, hot_n, hot_t, second_n = migrants(0, base_a)
    for k in range(MOMENTS):
        total(hot_t, k)
    half_wait(base_b, *pay_args)
    where_f, hot_f, hot_t, second_f = migrants(1, base_b)
    for k in range(4, MOMENTS):
        total(hot_t, k)
    for row in range(3):
        k = 4 + X_FACE[row]
        stress_send[0, row] = moments[k, pl.ds(0, Y), :]
        stress_send[1, row] = moments[k, pl.ds(pencils - Y, Y), :]
        k = 4 + Y_FACE[row]
        stress_send[2, row] = moments[k, pl.ds(0, X, stride=Y), :]
        stress_send[3, row] = moments[k, pl.ds(Y - 1, X, stride=Y), :]
    faces_start(*stress_args)
    for k in range(4):
        total(hot_t, k)

    lane = iota((pencils, Z), 1)

    def along_z(x, step):
        if step > 0:
            return jnp.where(lane == Z - 1, 0.0, pltpu.roll(x, Z - 1, 1))
        return jnp.where(lane == 0, 0.0, pltpu.roll(x, 1, 1))

    def fill(slot, value):
        wide[slot, 1 : X + 1, 8 : 8 + Y, :] = value.reshape(X, Y, Z)

    def edge_x(slot, halo, c):
        wide[slot, 0, 8 : 8 + Y, :] = halo[0, c]
        wide[slot, X + 1, 8 : 8 + Y, :] = halo[1, c]

    def edge_y(slot, halo, c):
        for x in range(X):
            wide[slot, x + 1, 7:8, :] = halo[2, c, x : x + 1]
            wide[slot, x + 1, 8 + Y : 9 + Y, :] = halo[3, c, x : x + 1]

    def along_x(slot, step):
        return wide[slot, 1 + step : 1 + step + X, 8 : 8 + Y, :].reshape(pencils, Z)

    def along_y(slot, step):
        return wide[slot, 1 : X + 1, 8 + step : 8 + step + Y, :].reshape(pencils, Z)

    faces_wait(*face_args)
    f = [flow[0], flow[1], flow[2], heat[...]]
    base = []
    for c in range(4):
        fill(c, f[c])
        edge_x(c, face_recv, c)
        edge_y(c, face_recv, c)
        smooth = along_x(c, 1) + along_x(c, -1) + along_y(c, 1) + along_y(c, -1)
        smooth = smooth + along_z(f[c], 1) + along_z(f[c], -1) - 6.0 * f[c]
        base.append(f[c] + VISCOSITY * smooth)
    density = moments[0]
    momentum = [moments[1 + c] for c in range(3)]
    for c in range(3):
        base[c] = base[c] + COUPLING * (momentum[c] - density * f[c])
    dots = momentum[0] * f[0] + momentum[1] * f[1] + momentum[2] * f[2]
    squares = f[0] * f[0] + f[1] * f[1] + f[2] * f[2]
    energy = (moments[4] + moments[7] + moments[9] - 2.0 * dots + density * squares) / 3.0
    fields_out[3] = base[3] + COUPLING * (energy - density * f[3])
    stress = [moments[4 + s] for s in range(6)]
    for s in range(5):
        fill(4 + s, stress[s])
    for row in range(3):
        sz = stress[PAIR_INDEX[row][2]]
        base[row] = base[row] - (0.5 * STRESS_GAIN) * (along_z(sz, 1) - along_z(sz, -1))

    faces_wait(*stress_args)
    for row in range(3):
        edge_x(4 + X_FACE[row], stress_recv, row)
        edge_y(4 + Y_FACE[row], stress_recv, row)
    fresh = []
    for row in range(3):
        sx, sy = 4 + X_FACE[row], 4 + Y_FACE[row]
        slope = along_x(sx, 1) - along_x(sx, -1) + along_y(sy, 1) - along_y(sy, -1)
        value = base[row] - (0.5 * STRESS_GAIN) * slope
        fields_out[row] = value
        fresh.append(jnp.concatenate(split(value), axis=0))

    for base, where_a, hot, second_a in (
        (base_a, where_n, hot_n, second_n),
        (base_b, where_f, hot_f, second_f),
    ):
        for c in range(3):
            w = lanes(dot(hot, fresh[c]), where_a)
            third = second_a[c] + RELAXATION * (w - second_a[c])
            for j in range(cap):
                back_send[pl.ds(base * back_rows + c * cap + j, n // 2, stride=back_rows), :] = third[
                    j * (n // 2) : (j + 1) * (n // 2)
                ]
    all_start(others, *back_args)
    own = pl.ds(pl.multiple_of(me * back_rows, 8), back_rows)
    back_recv[own, :] = back_send[own, :]
    for c in range(3):
        w = lanes(dot(home_hot, fresh[c]), where)
        now = second_ref[c]
        second_ref[c] = live * (now + RELAXATION * (w - now))
    all_wait(others, *back_args)
    for c in range(3):
        returned = jnp.concatenate(
            [back_recv[pl.ds(c * cap + j, n, stride=back_rows), :] for j in range(cap)], axis=0
        )
        speed_out[c] = jnp.where(moved, live * pick(to_block, returned), second_ref[c])

    all_sent(far + near, *pay_args)
    faces_sent(*face_args)
    faces_sent(*stress_args)
    all_sent(others, *back_args)


def put_out(fields, velocity, fields_out, velocity_out, sems):
    copies = (
        pltpu.make_async_copy(fields, fields_out, sems.at[0]),
        pltpu.make_async_copy(velocity, velocity_out, sems.at[1]),
    )
    for copy in copies:
        copy.start()
    for copy in copies:
        copy.wait()


def shards(
    flow_speed_field,
    thermal_field,
    walker_speed_vectors,
    walker_statistical_mass,
    gaussian_samples,
    walker_strip_position,
    group_active_tally,
    group_resident_strip,
    migrating_group_table,
    target_processor_slot,
    entered_strip_slot,
):
    n = lax.axis_size("yz")
    n_gx = lax.axis_size("gx")
    X, Y, Z = thermal_field.shape
    blocks, slots = walker_statistical_mass.shape
    moving = migrating_group_table.shape[0]
    cap = 2 * moving // n
    received = n * cap
    rows = -(-(SENT * cap + 1) // 8) * 8
    back_rows = -(-3 * cap // 8) * 8
    operands = (
        flow_speed_field.reshape(3, X * Y, Z),
        thermal_field.reshape(X * Y, Z),
        walker_speed_vectors,
        walker_statistical_mass,
        gaussian_samples.reshape(6, blocks, slots),
        walker_strip_position,
        group_active_tally.reshape(1, blocks),
        group_resident_strip.reshape(1, blocks),
        migrating_group_table.reshape(1, moving),
        target_processor_slot.reshape(1, moving),
        entered_strip_slot.reshape(1, moving),
    )
    vmem = pl.BlockSpec(memory_space=pltpu.VMEM)
    fields, velocity = pl.pallas_call(
        functools.partial(kernel, n, n_gx, (X, Y, Z)),
        out_shape=(
            pltpu.VMEM((4, X * Y, Z), F32),
            pltpu.VMEM((3, blocks, slots), F32),
        ),
        in_specs=[pl.BlockSpec(memory_space=pltpu.HBM)] * 11,
        out_specs=(vmem, vmem),
        scratch_shapes=[pltpu.VMEM(x.shape, x.dtype) for x in operands]
        + [pltpu.SemaphoreType.DMA((11,))]
        + [
            pltpu.VMEM((max(blocks, received) * PITCH, slots), F32),
            pltpu.VMEM((max(blocks, received) // 2 * PITCH, Z), F32),
            pltpu.VMEM((3, blocks, slots), F32),
            pltpu.VMEM((2, received // 2, slots), jnp.int32),
            pltpu.VMEM((MOMENTS, X * Y, Z), F32),
            pltpu.VMEM((9, X + 2, 24, Z), F32),
            pltpu.VMEM((4, 4, 8, Z), F32),
            pltpu.VMEM((4, 4, 8, Z), F32),
            pltpu.VMEM((4, 3, 8, Z), F32),
            pltpu.VMEM((4, 3, 8, Z), F32),
            pltpu.VMEM((n * rows, slots), F32),
            pltpu.VMEM((n * rows, slots), F32),
            pltpu.VMEM((n * back_rows, slots), F32),
            pltpu.VMEM((n * back_rows, slots), F32),
            pltpu.SemaphoreType.DMA((n,)),
            pltpu.SemaphoreType.DMA((n,)),
            pltpu.SemaphoreType.DMA((4,)),
            pltpu.SemaphoreType.DMA((4,)),
            pltpu.SemaphoreType.DMA((4,)),
            pltpu.SemaphoreType.DMA((4,)),
            pltpu.SemaphoreType.DMA((n,)),
            pltpu.SemaphoreType.DMA((n,)),
        ],
        compiler_params=pltpu.CompilerParams(
            collective_id=0, has_side_effects=True, vmem_limit_bytes=32 * 1024 * 1024
        ),
    )(*(pltpu.with_memory_space_constraint(x, pltpu.HBM) for x in operands))
    hbm = pl.BlockSpec(memory_space=pltpu.HBM)
    fields, velocity = pl.pallas_call(
        put_out,
        out_shape=(
            jax.ShapeDtypeStruct((4, X * Y, Z), F32),
            jax.ShapeDtypeStruct((3, blocks, slots), F32),
        ),
        in_specs=[vmem, vmem],
        out_specs=(hbm, hbm),
        scratch_shapes=[pltpu.SemaphoreType.DMA((2,))],
        compiler_params=pltpu.CompilerParams(vmem_limit_bytes=32 * 1024 * 1024),
    )(fields, velocity)
    return fields.reshape(4, X, Y, Z), velocity


def solution(mesh):
    return jax.shard_map(
        shards,
        mesh=mesh,
        in_specs=(
            P(None, "gx", "yz", None),
            P("gx", "yz", None),
            P(None, ("gx", "yz"), None),
            P(("gx", "yz"), None),
            P(None, None, ("gx", "yz"), None),
            P(("gx", "yz"), None),
            P(("gx", "yz")),
            P(("gx", "yz")),
            P(("gx", "yz")),
            P(("gx", "yz"), None),
            P(("gx", "yz")),
        ),
        out_specs=(P(None, "gx", "yz", None), P(None, ("gx", "yz"), None)),
        check_vma=False,
    )
```

```python
import functools
import math

import jax
import jax.numpy as jnp
from jax import lax
from jax.experimental import pallas as pl
from jax.experimental.pallas import tpu as pltpu
from jax.sharding import PartitionSpec as P

DECAY = 0.6
VISCOSITY = 0.05
COUPLING = 0.02
STRESS_GAIN = 0.005
RELAXATION = 0.5
PAIRS = ((0, 0), (0, 1), (0, 2), (1, 1), (1, 2), (2, 2))
PAIR_INDEX = ((0, 1, 2), (1, 3, 4), (2, 4, 5))
MOMENTS = 10
PITCH = 24
SENT = 8
UNROLL = 16
LOADS = ((8,), (9,), (10,), (7,), (6,), (0, 1, 5, 3), (4, 2))
X_FACE = tuple(row[0] for row in PAIR_INDEX)
Y_FACE = tuple(row[1] for row in PAIR_INDEX)
MESH = pl.DeviceIdType.MESH
BF16 = jnp.bfloat16
F32 = jnp.float32


def split(x):
    high = x.astype(BF16)
    return high, (x - high.astype(F32)).astype(BF16)


def dot(a, b):
    return jnp.dot(a, b, preferred_element_type=F32)


def dot_last(a, b):
    return lax.dot_general(a, b, (((1,), (1,)), ((), ())), preferred_element_type=F32)


def twice(x, axis):
    return jnp.concatenate([x, x], axis=axis)


def pick(onehot_twice, x):
    return dot(onehot_twice, jnp.concatenate(split(x), axis=0))


def lanes(x, index):
    return jnp.take_along_axis(x, index, axis=1, mode="promise_in_bounds")


def onehot(condition):
    return jnp.where(condition, 1.0, 0.0)


def partner(me, i, n):
    peer, bit = 0, 1
    while bit < n:
        own = lax.rem(lax.div(me, bit), 2)
        peer = peer + bit * (1 - own if i & bit else own)
        bit *= 2
    return peer


def drift(start, u, spread, noise):
    return u + DECAY * (start - u) + spread * noise


def deposit(count, v_ref, cells_ref, pb_ref, first=0, last=None):
    width = v_ref.shape[1]
    slots = cells_ref.shape[1]
    half = count // 2
    unroll = math.gcd(half, UNROLL)
    where = lax.broadcasted_iota(jnp.int32, (width, slots), 0)
    none = jnp.zeros((8, slots), F32)
    mine = lax.broadcasted_iota(jnp.int32, (8, slots), 0) < MOMENTS - 8

    def some(step, carry):
        for t in range(unroll):
            n = step * unroll + t
            start = pl.multiple_of(n * 2 * PITCH, 2 * PITCH)
            rows = [v_ref[pl.ds(start + 8 * part, 8), :] for part in range(6)]
            left = [rows[0], jnp.where(mine, rows[1], 0.0), none, rows[3], jnp.where(mine, rows[4], 0.0), none]
            right = [none, jnp.where(mine, 0.0, rows[1]), rows[2], none, jnp.where(mine, 0.0, rows[4]), rows[5]]
            lhs = jnp.concatenate(
                [jnp.concatenate(side, axis=0).astype(BF16) for side in (left, right)], axis=1
            )
            hot = jnp.concatenate(
                [onehot(cells_ref[pl.ds(n + block, 1), :] == where).astype(BF16) for block in (0, half)], axis=1
            )
            out = dot_last(lhs, hot)
            pb_ref[pl.ds(pl.multiple_of(n * PITCH, 8), PITCH), :] = out[:PITCH] + out[PITCH:]
        return carry

    lax.fori_loop(first, half // unroll if last is None else last, some, 0)


def put_terms(v_ref, count, weight, second):
    half = count // 2
    weighted = [weight * second[row] for row in range(3)]
    terms = [weight] + weighted + [weighted[one] * second[two] for one, two in PAIRS]
    for k, term in enumerate(terms):
        high = term.astype(BF16).astype(F32)
        for part, value in enumerate((high, term - high)):
            for block in range(2):
                v_ref[pl.ds(part * PITCH + block * MOMENTS + k, half, stride=2 * PITCH), :] = value[
                    block * half : (block + 1) * half
                ]


def deposited(pb_ref, count, k):
    half = count // 2
    return jnp.concatenate(
        [pb_ref[pl.ds(block * MOMENTS + k, half, stride=PITCH), :] for block in range(2)], axis=0
    )


def kernel(
    n,
    n_gx,
    spans,
    *refs,
):
    sources, (fields_out, speed_out), held, load_s = refs[:11], refs[11:13], refs[13:24], refs[24]
    flow, heat, speed, mass, noise, cells, tally, home, table, target, entered = held
    (
    v_ref,
    pb_ref,
    second_ref,
    cells_a,
    moments,
    wide,
    zeros,
    face_send,
    face_recv,
    stress_send,
    stress_recv,
    out_ref,
    in_ref,
    back_send,
    back_recv,
    sent_s,
    out_r,
    face_r,
    stress_r,
    back_r,
    ) = refs[25:]
    loads = [
        pltpu.make_async_copy(source, kept, load_s.at[[i in batch for batch in LOADS].index(True)])
        for i, (source, kept) in enumerate(zip(sources, held))
    ]
    X, Y, Z = spans
    pencils = X * Y
    blocks, slots = mass.shape
    moving = table.shape[1]
    cap = 2 * moving // n
    received = n * cap
    rows = out_ref.shape[0] // n
    back_rows = back_send.shape[0] // n
    gx = lax.axis_index("gx")
    me = lax.axis_index("yz")
    far = [partner(me, i, n) for i in range(n - 1, n // 2 - 1, -1)]
    near = [partner(me, i, n) for i in range(n // 2 - 1, 0, -1)]
    odd = lax.rem(gx, 2)
    turns = [j + odd * (n - 2 - 2 * j) for j in range(n - 1)]
    others = [j + lax.div(j + n - me, n) for j in turns]
    group = received // 2
    half_a = jnp.minimum(lax.div(me, n // 4), 1)
    half_b = 1 - half_a
    base_a, base_b = half_a * (n // 2), half_b * (n // 2)
    for batch in LOADS:
        for i in batch:
            loads[i].start()

    barrier = pltpu.get_barrier_semaphore()
    for peer in far + near:
        pl.semaphore_signal(barrier, inc=1, device_id={"yz": peer}, device_id_type=MESH)

    @pl.when(gx > 0)
    def _():
        pl.semaphore_signal(barrier, inc=1, device_id={"gx": gx - 1}, device_id_type=MESH)

    @pl.when(gx < n_gx - 1)
    def _():
        pl.semaphore_signal(barrier, inc=1, device_id={"gx": gx + 1}, device_id_type=MESH)

    sides = (
        (0, 1, gx > 0, gx == 0, {"gx": gx - 1}),
        (1, 0, gx < n_gx - 1, gx == n_gx - 1, {"gx": gx + 1}),
        (2, 3, me > 0, me == 0, {"yz": me - 1}),
        (3, 2, me < n - 1, me == n - 1, {"yz": me + 1}),
    )
    def face_copy(side, other, where, send, recv, send_sem, recv_sem):
        return pltpu.make_async_remote_copy(
            src_ref=send.at[side],
            dst_ref=recv.at[other],
            send_sem=send_sem.at[1],
            recv_sem=recv_sem.at[0],
            device_id=where,
            device_id_type=MESH,
        )

    def faces_start(send, recv, send_sem, recv_sem):
        for side, other, there, edge, where in sides:

            @pl.when(there)
            def _(side=side, other=other, where=where):
                face_copy(side, other, where, send, recv, send_sem, recv_sem).start()

            @pl.when(edge)
            def _(side=side):
                pltpu.make_async_copy(
                    zeros.at[pl.ds(0, recv.shape[1])], recv.at[side], recv_sem.at[0]
                ).start()

    def faces_wait(send, recv, send_sem, recv_sem):
        arrived(math.prod(recv.shape[:-1]), v_ref, recv_sem.at[0])

    face_args = (face_send, face_recv, sent_s, face_r)
    stress_args = (stress_send, stress_recv, sent_s, stress_r)

    def all_copy(peer, source, send, recv, height, pitch, parts, send_sem, recv_sem):
        return pltpu.make_async_remote_copy(
            src_ref=send.at[pl.ds(pl.multiple_of(peer * pitch, 8), height), :],
            dst_ref=recv.at[pl.ds(pl.multiple_of(source * pitch, 8), height), :],
            send_sem=send_sem.at[0],
            recv_sem=recv_sem.at[lax.div(source * parts, n)],
            device_id={"yz": peer},
            device_id_type=MESH,
        )

    def all_start(peers, *args):
        for peer in peers:
            all_copy(peer, me, *args).start()

    def own_copy(send, recv, height, pitch, parts, send_sem, recv_sem):
        own = pl.ds(pl.multiple_of(me * pitch, 8), height)
        return pltpu.make_async_copy(send.at[own, :], recv.at[own, :], recv_sem.at[lax.div(me * parts, n)])

    def all_wait(part, send, recv, height, pitch, parts, send_sem, recv_sem):
        arrived(n // parts * height, v_ref, recv_sem.at[part])

    pay_args = (out_ref, in_ref, SENT * cap + 1, rows, 2, sent_s, out_r)
    back_args = (back_send, back_recv, 3 * cap, back_rows, 1, sent_s, back_r)

    def arrived(count, buffer, sem):
        rows = buffer.at[pl.ds(0, count), :]
        pltpu.make_async_copy(rows, rows, sem).wait()

    def landed(batch):
        arrived(sum(math.prod(held[i].shape[:-1]) for i in LOADS[batch]), v_ref, load_s.at[batch])

    zeros[...] = jnp.zeros(zeros.shape, F32)

    for batch in range(5):
        loads[LOADS[batch][0]].wait()
    iota = functools.partial(lax.broadcasted_iota, jnp.int32)

    def folded(shape, axis, period):
        place = iota(shape, axis)
        return jnp.where(place < period, place, place - period)

    eye = iota((moving, moving), 0) == iota((moving, moving), 1)
    target_row = target[...]
    target_col = jnp.sum(jnp.where(eye, target_row, 0), axis=1, keepdims=True)
    earlier = (target_col == target_row) & (iota((moving, moving), 0) < iota((moving, moving), 1))
    rank = jnp.sum(jnp.where(earlier, 1, 0), axis=0, keepdims=True)
    slot_row = rank * n + target_row
    slot_hot = onehot(folded((2 * received, moving), 0, received) == slot_row)
    block_hot = onehot(iota((blocks, moving), 0) == table[...]).astype(BF16)
    from_block = dot_last(slot_hot[:received].astype(BF16), block_hot).astype(BF16)
    from_twice = twice(from_block, 1)
    to_block = dot_last(block_hot, slot_hot.astype(BF16))
    moved = jnp.sum(to_block, axis=1, keepdims=True) > 0.5
    to_block = to_block.astype(BF16)
    pencil_out = jnp.sum(slot_hot[:received] * entered[...].astype(F32), axis=1, keepdims=True)

    home_t = onehot(folded((2 * pencils, blocks), 0, pencils) == home[...])
    home_hot = home_t.T.astype(BF16)
    home_t = twice(home_t[:pencils].astype(BF16), 1)
    live = onehot(iota((slots, blocks), 0) < tally[...]).T

    landed(5)
    u = [pick(home_hot, flow[c]) for c in range(3)]
    temp = pick(home_hot, heat[...])
    for c in range(4):
        grid = flow.at[c] if c < 3 else heat
        face_send[0, c] = grid[pl.ds(0, Y), :]
        face_send[1, c] = grid[pl.ds((X - 1) * Y, Y), :]
        face_send[2, c] = grid[pl.ds(0, X, stride=Y), :]
        face_send[3, c] = grid[pl.ds(Y - 1, X, stride=Y), :]

    where = cells[...]
    u = [lanes(u[c], where) for c in range(3)]
    spread = jnp.sqrt((1.0 - DECAY * DECAY) * lanes(temp, where))
    weight = mass[...] * live

    def send_row(c, value):
        for j in range(cap):
            out_ref[pl.ds(c * cap + j, n, stride=rows), :] = value[j * n : (j + 1) * n]

    send_row(6, pick(from_twice, weight))
    send_row(7, dot(from_block, where.astype(F32).astype(BF16)))
    place = lax.div(iota((n, slots), 1), slots // cap)
    pencil_row = jnp.broadcast_to(pencil_out[:n], (n, slots))
    for j in range(1, cap):
        pencil_row = jnp.where(place == j, pencil_out[j * n : (j + 1) * n], pencil_row)
    out_ref[pl.ds(SENT * cap, n, stride=rows), :] = pencil_row

    landed(6)
    for c in range(3):
        send_row(3 + c, pick(from_twice, noise[3 + c]))

    first = [drift(speed[c], u[c], spread, noise[c]) for c in range(3)]
    for c in range(3):
        send_row(c, pick(from_twice, first[c]))

    near_gx = jnp.where(gx > 0, 1, 0) + jnp.where(gx < n_gx - 1, 1, 0)
    neighbours = near_gx + jnp.where(me > 0, 1, 0) + jnp.where(me < n - 1, 1, 0)
    pl.semaphore_wait(barrier, n - 1 + near_gx)
    late = lax.rem(gx, 2) == 1

    @pl.when(jnp.logical_not(late))
    def _():
        all_start(far + near, *pay_args)

    faces_start(*face_args)
    own_copy(*pay_args).start()

    second = [drift(first[c], u[c], spread, noise[3 + c]) for c in range(3)]
    for c in range(3):
        second_ref[c] = second[c]
    put_terms(v_ref, blocks, jnp.where(moved, 0.0, weight), second)
    deposit(blocks, v_ref, cells, pb_ref, 0, 3)

    @pl.when(late)
    def _():
        all_start(far + near, *pay_args)

    deposit(blocks, v_ref, cells, pb_ref, 3)
    for k in range(MOMENTS):
        moments[k] = pick(home_t, deposited(pb_ref, blocks, k))

    def migrants(side, base):
        def taken(row):
            return in_ref[pl.ds(base * rows + row, n // 2, stride=rows), :]

        got = [jnp.concatenate([taken(c * cap + j) for j in range(cap)], axis=0) for c in range(SENT)]
        where = got[7].astype(jnp.int32)
        cells_a[side] = where
        pencil_row = taken(SENT * cap)
        pencil = jnp.concatenate(
            [lanes(pencil_row, jnp.full((n // 2, slots), j * (slots // cap), jnp.int32)) for j in range(cap)], axis=0
        ).astype(jnp.int32)
        hot = onehot(pencil[:, : 2 * pencils] == folded((group, 2 * pencils), 1, pencils))
        narrow = hot[:, :pencils]
        hot = hot.astype(BF16)
        u = [lanes(pick(hot, flow[c]), where) for c in range(3)]
        spread = jnp.sqrt((1.0 - DECAY * DECAY) * lanes(pick(hot, heat[...]), where))
        second = [drift(got[c], u[c], spread, got[3 + c]) for c in range(3)]
        put_terms(v_ref.at[pl.ds(side * group * PITCH, group * PITCH), :], group, got[6], second)
        deposit(
            group,
            v_ref.at[pl.ds(side * group * PITCH, group * PITCH), :],
            cells_a.at[side],
            pb_ref.at[pl.ds(side * group // 2 * PITCH, group // 2 * PITCH), :],
        )
        return where, hot, narrow, second

    all_wait(half_a, *pay_args)
    where_n, hot_n, narrow_n, second_n = migrants(0, base_a)
    all_wait(half_b, *pay_args)
    where_f, hot_f, narrow_f, second_f = migrants(1, base_b)
    hot_t = twice(jnp.concatenate([narrow_n, narrow_f], axis=0), 0).T.astype(BF16)

    def total(k):
        parts = [
            deposited(pb_ref.at[pl.ds(side * group // 2 * PITCH, group // 2 * PITCH), :], group, k) for side in range(2)
        ]
        moments[k] = moments[k] + pick(hot_t, jnp.concatenate(parts, axis=0))

    for k in range(4, MOMENTS):
        total(k)
    for row in range(3):
        k = 4 + X_FACE[row]
        stress_send[0, row] = moments[k, pl.ds(0, Y), :]
        stress_send[1, row] = moments[k, pl.ds(pencils - Y, Y), :]
        k = 4 + Y_FACE[row]
        stress_send[2, row] = moments[k, pl.ds(0, X, stride=Y), :]
        stress_send[3, row] = moments[k, pl.ds(Y - 1, X, stride=Y), :]
    faces_start(*stress_args)
    for k in range(4):
        total(k)

    lane = iota((pencils, Z), 1)

    def along_z(x, step):
        if step > 0:
            return jnp.where(lane == Z - 1, 0.0, pltpu.roll(x, Z - 1, 1))
        return jnp.where(lane == 0, 0.0, pltpu.roll(x, 1, 1))

    def fill(slot, value):
        wide[slot, 1 : X + 1, 8 : 8 + Y, :] = value.reshape(X, Y, Z)

    def edge_x(slot, halo, c):
        wide[slot, 0, 8 : 8 + Y, :] = halo[0, c]
        wide[slot, X + 1, 8 : 8 + Y, :] = halo[1, c]

    def edge_y(slot, halo, c):
        for x in range(X):
            wide[slot, x + 1, 7:8, :] = halo[2, c, x : x + 1]
            wide[slot, x + 1, 8 + Y : 9 + Y, :] = halo[3, c, x : x + 1]

    def along_x(slot, step):
        return wide[slot, 1 + step : 1 + step + X, 8 : 8 + Y, :].reshape(pencils, Z)

    def along_y(slot, step):
        return wide[slot, 1 : X + 1, 8 + step : 8 + step + Y, :].reshape(pencils, Z)

    faces_wait(*face_args)
    f = [flow[0], flow[1], flow[2], heat[...]]
    base = []
    for c in range(4):
        fill(c, f[c])
        edge_x(c, face_recv, c)
        edge_y(c, face_recv, c)
        smooth = along_x(c, 1) + along_x(c, -1) + along_y(c, 1) + along_y(c, -1)
        smooth = smooth + along_z(f[c], 1) + along_z(f[c], -1) - 6.0 * f[c]
        base.append(f[c] + VISCOSITY * smooth)
    density = moments[0]
    momentum = [moments[1 + c] for c in range(3)]
    for c in range(3):
        base[c] = base[c] + COUPLING * (momentum[c] - density * f[c])
    dots = momentum[0] * f[0] + momentum[1] * f[1] + momentum[2] * f[2]
    squares = f[0] * f[0] + f[1] * f[1] + f[2] * f[2]
    energy = (moments[4] + moments[7] + moments[9] - 2.0 * dots + density * squares) / 3.0
    fields_out[3] = base[3] + COUPLING * (energy - density * f[3])
    stress = [moments[4 + s] for s in range(6)]
    for s in range(5):
        fill(4 + s, stress[s])
    for row in range(3):
        sz = stress[PAIR_INDEX[row][2]]
        base[row] = base[row] - (0.5 * STRESS_GAIN) * (along_z(sz, 1) - along_z(sz, -1))

    faces_wait(*stress_args)
    for row in range(3):
        edge_x(4 + X_FACE[row], stress_recv, row)
        edge_y(4 + Y_FACE[row], stress_recv, row)
    fresh = []
    for row in range(3):
        sx, sy = 4 + X_FACE[row], 4 + Y_FACE[row]
        slope = along_x(sx, 1) - along_x(sx, -1) + along_y(sy, 1) - along_y(sy, -1)
        value = base[row] - (0.5 * STRESS_GAIN) * slope
        fields_out[row] = value
        fresh.append(jnp.concatenate(split(value), axis=0))

    for base, where_a, hot, second_a in (
        (base_a, where_n, hot_n, second_n),
        (base_b, where_f, hot_f, second_f),
    ):
        for c in range(3):
            w = lanes(dot(hot, fresh[c]), where_a)
            third = second_a[c] + RELAXATION * (w - second_a[c])
            for j in range(cap):
                back_send[pl.ds(base * back_rows + c * cap + j, n // 2, stride=back_rows), :] = third[
                    j * (n // 2) : (j + 1) * (n // 2)
                ]
    all_start(others, *back_args)
    own_copy(*back_args).start()
    for c in range(3):
        w = lanes(dot(home_hot, fresh[c]), where)
        now = second_ref[c]
        second_ref[c] = live * (now + RELAXATION * (w - now))
    all_wait(0, *back_args)
    for c in range(3):
        returned = jnp.concatenate(
            [back_recv[pl.ds(c * cap + j, n, stride=back_rows), :] for j in range(cap)], axis=0
        )
        speed_out[c] = jnp.where(moved, live * pick(to_block, returned), second_ref[c])

    arrived((n - 1) * (pay_args[2] + back_args[2]), v_ref, sent_s.at[0])
    for count in range(1, 5):

        @pl.when(neighbours == count)
        def _(count=count):
            arrived(count * sum(math.prod(x.shape[1:-1]) for x in (face_send, stress_send)), v_ref, sent_s.at[1])


def put_out(fields, velocity, fields_out, velocity_out, sems):
    copies = (
        pltpu.make_async_copy(fields, fields_out, sems.at[0]),
        pltpu.make_async_copy(velocity, velocity_out, sems.at[1]),
    )
    for copy in copies:
        copy.start()
    for copy in copies:
        copy.wait()


def shards(
    flow_speed_field,
    thermal_field,
    walker_speed_vectors,
    walker_statistical_mass,
    gaussian_samples,
    walker_strip_position,
    group_active_tally,
    group_resident_strip,
    migrating_group_table,
    target_processor_slot,
    entered_strip_slot,
):
    n = lax.axis_size("yz")
    n_gx = lax.axis_size("gx")
    X, Y, Z = thermal_field.shape
    blocks, slots = walker_statistical_mass.shape
    moving = migrating_group_table.shape[0]
    cap = 2 * moving // n
    received = n * cap
    rows = -(-(SENT * cap + 1) // 8) * 8
    back_rows = -(-3 * cap // 8) * 8
    operands = (
        flow_speed_field.reshape(3, X * Y, Z),
        thermal_field.reshape(X * Y, Z),
        walker_speed_vectors,
        walker_statistical_mass,
        gaussian_samples.reshape(6, blocks, slots),
        walker_strip_position,
        group_active_tally.reshape(1, blocks),
        group_resident_strip.reshape(1, blocks),
        migrating_group_table.reshape(1, moving),
        target_processor_slot.reshape(1, moving),
        entered_strip_slot.reshape(1, moving),
    )
    vmem = pl.BlockSpec(memory_space=pltpu.VMEM)
    fields, velocity = pl.pallas_call(
        functools.partial(kernel, n, n_gx, (X, Y, Z)),
        out_shape=(
            pltpu.VMEM((4, X * Y, Z), F32),
            pltpu.VMEM((3, blocks, slots), F32),
        ),
        in_specs=[pl.BlockSpec(memory_space=pltpu.HBM)] * 11,
        out_specs=(vmem, vmem),
        scratch_shapes=[pltpu.VMEM(x.shape, x.dtype) for x in operands]
        + [pltpu.SemaphoreType.DMA((len(LOADS),))]
        + [
            pltpu.VMEM((max(blocks, received) * PITCH, slots), F32),
            pltpu.VMEM((max(blocks, received) // 2 * PITCH, Z), F32),
            pltpu.VMEM((3, blocks, slots), F32),
            pltpu.VMEM((2, received // 2, slots), jnp.int32),
            pltpu.VMEM((MOMENTS, X * Y, Z), F32),
            pltpu.VMEM((9, X + 2, 24, Z), F32),
            pltpu.VMEM((4, 8, Z), F32),
            pltpu.VMEM((4, 4, 8, Z), F32),
            pltpu.VMEM((4, 4, 8, Z), F32),
            pltpu.VMEM((4, 3, 8, Z), F32),
            pltpu.VMEM((4, 3, 8, Z), F32),
            pltpu.VMEM((n * rows, slots), F32),
            pltpu.VMEM((n * rows, slots), F32),
            pltpu.VMEM((n * back_rows, slots), F32),
            pltpu.VMEM((n * back_rows, slots), F32),
            pltpu.SemaphoreType.DMA((2,)),
            pltpu.SemaphoreType.DMA((2,)),
            pltpu.SemaphoreType.DMA((1,)),
            pltpu.SemaphoreType.DMA((1,)),
            pltpu.SemaphoreType.DMA((1,)),
        ],
        compiler_params=pltpu.CompilerParams(
            collective_id=0, has_side_effects=True, vmem_limit_bytes=32 * 1024 * 1024
        ),
    )(*(pltpu.with_memory_space_constraint(x, pltpu.HBM) for x in operands))
    hbm = pl.BlockSpec(memory_space=pltpu.HBM)
    fields, velocity = pl.pallas_call(
        put_out,
        out_shape=(
            jax.ShapeDtypeStruct((4, X * Y, Z), F32),
            jax.ShapeDtypeStruct((3, blocks, slots), F32),
        ),
        in_specs=[vmem, vmem],
        out_specs=(hbm, hbm),
        scratch_shapes=[pltpu.SemaphoreType.DMA((2,))],
        compiler_params=pltpu.CompilerParams(vmem_limit_bytes=32 * 1024 * 1024),
    )(fields, velocity)
    return fields.reshape(4, X, Y, Z), velocity


def solution(mesh):
    return jax.shard_map(
        shards,
        mesh=mesh,
        in_specs=(
            P(None, "gx", "yz", None),
            P("gx", "yz", None),
            P(None, ("gx", "yz"), None),
            P(("gx", "yz"), None),
            P(None, None, ("gx", "yz"), None),
            P(("gx", "yz"), None),
            P(("gx", "yz")),
            P(("gx", "yz")),
            P(("gx", "yz")),
            P(("gx", "yz"), None),
            P(("gx", "yz")),
        ),
        out_specs=(P(None, "gx", "yz", None), P(None, ("gx", "yz"), None)),
        check_vma=False,
    )
```

```python
import functools
import math

import jax
import jax.numpy as jnp
from jax import lax
from jax.experimental import pallas as pl
from jax.experimental.pallas import tpu as pltpu
from jax.sharding import PartitionSpec as P

DECAY = 0.6
VISCOSITY = 0.05
COUPLING = 0.02
STRESS_GAIN = 0.005
RELAXATION = 0.5
PAIRS = ((0, 0), (0, 1), (0, 2), (1, 1), (1, 2), (2, 2))
PAIR_INDEX = ((0, 1, 2), (1, 3, 4), (2, 4, 5))
MOMENTS = 10
PITCH = 24
PAIR_PITCH = 56
SENT = 8
UNROLL = 16
LOADS = ((8,), (9,), (10,), (7,), (6,), (0, 1, 5, 3), (4, 2))
X_FACE = tuple(row[0] for row in PAIR_INDEX)
Y_FACE = tuple(row[1] for row in PAIR_INDEX)
MESH = pl.DeviceIdType.MESH
BF16 = jnp.bfloat16
F32 = jnp.float32


def split(x):
    high = x.astype(BF16)
    return high, (x - high.astype(F32)).astype(BF16)


def dot(a, b):
    return jnp.dot(a, b, preferred_element_type=F32)


def dot_last(a, b):
    return lax.dot_general(a, b, (((1,), (1,)), ((), ())), preferred_element_type=F32)


def twice(x, axis):
    return jnp.concatenate([x, x], axis=axis)


def pick(onehot_twice, x):
    return dot(onehot_twice, jnp.concatenate(split(x), axis=0))


def lanes(x, index):
    return jnp.take_along_axis(x, index, axis=1, mode="promise_in_bounds")


def onehot(condition):
    return jnp.where(condition, 1.0, 0.0)


def partner(me, i, n):
    peer, bit = 0, 1
    while bit < n:
        own = lax.rem(lax.div(me, bit), 2)
        peer = peer + bit * (1 - own if i & bit else own)
        bit *= 2
    return peer


def drift(start, u, spread, noise):
    return u + DECAY * (start - u) + spread * noise


def deposit(count, v_ref, cells_ref, pb_ref):
    width = v_ref.shape[1]
    slots = cells_ref.shape[1]
    half = count // 2
    unroll = math.gcd(half, UNROLL)
    where = lax.broadcasted_iota(jnp.int32, (width, slots), 0)
    none = jnp.zeros((8, slots), F32)
    mine = lax.broadcasted_iota(jnp.int32, (8, slots), 0) < MOMENTS - 8

    def some(step, carry):
        for t in range(unroll):
            n = step * unroll + t
            start = pl.multiple_of(n * PAIR_PITCH, 8)
            rows = [v_ref[pl.ds(start + 8 * part, 8), :] for part in range(6)]
            left = [rows[0], jnp.where(mine, rows[1], 0.0), none, rows[3], jnp.where(mine, rows[4], 0.0), none]
            right = [none, jnp.where(mine, 0.0, rows[1]), rows[2], none, jnp.where(mine, 0.0, rows[4]), rows[5]]
            lhs = jnp.concatenate(
                [jnp.concatenate(side, axis=0).astype(BF16) for side in (left, right)], axis=1
            )
            hot = jnp.concatenate(
                [onehot(cells_ref[pl.ds(n + block, 1), :] == where).astype(BF16) for block in (0, half)], axis=1
            )
            out = dot_last(lhs, hot)
            pb_ref[pl.ds(pl.multiple_of(n * PITCH, 8), PITCH), :] = out[:PITCH] + out[PITCH:]
        return carry

    lax.fori_loop(0, half // unroll, some, 0)


def put_terms(v_ref, count, weight, second):
    half = count // 2
    weighted = [weight * second[row] for row in range(3)]
    terms = [weight] + weighted + [weighted[one] * second[two] for one, two in PAIRS]
    for k, term in enumerate(terms):
        high = term.astype(BF16).astype(F32)
        for part, value in enumerate((high, term - high)):
            for block in range(2):
                v_ref[pl.ds(part * PITCH + block * MOMENTS + k, half, stride=PAIR_PITCH), :] = value[
                    block * half : (block + 1) * half
                ]


def deposited(pb_ref, count, k):
    half = count // 2
    return jnp.concatenate(
        [pb_ref[pl.ds(block * MOMENTS + k, half, stride=PITCH), :] for block in range(2)], axis=0
    )


def kernel(
    n,
    n_gx,
    spans,
    *refs,
):
    sources, (fields_out, speed_out), held, load_s = refs[:11], refs[11:13], refs[13:24], refs[24]
    flow, heat, speed, mass, noise, cells, tally, home, table, target, entered = held
    (
    v_ref,
    pb_ref,
    second_ref,
    cells_a,
    moments,
    wide,
    zeros,
    face_send,
    face_recv,
    stress_send,
    stress_recv,
    out_ref,
    in_ref,
    back_send,
    back_recv,
    sent_s,
    out_r,
    face_r,
    stress_r,
    back_r,
    ) = refs[25:]
    loads = [
        pltpu.make_async_copy(source, kept, load_s.at[[i in batch for batch in LOADS].index(True)])
        for i, (source, kept) in enumerate(zip(sources, held))
    ]
    X, Y, Z = spans
    pencils = X * Y
    blocks, slots = mass.shape
    moving = table.shape[1]
    cap = 2 * moving // n
    received = n * cap
    rows = out_ref.shape[0] // n
    back_rows = back_send.shape[0] // n
    gx = lax.axis_index("gx")
    me = lax.axis_index("yz")
    far = [partner(me, i, n) for i in range(n - 1, n // 2 - 1, -1)]
    near = [partner(me, i, n) for i in range(n // 2 - 1, 0, -1)]
    odd = lax.rem(gx, 2)
    turns = [j + odd * (n - 2 - 2 * j) for j in range(n - 1)]
    others = [j + lax.div(j + n - me, n) for j in turns]
    group = received // 2
    half_a = jnp.minimum(lax.div(me, n // 4), 1)
    half_b = 1 - half_a
    base_a, base_b = half_a * (n // 2), half_b * (n // 2)
    for batch in LOADS:
        for i in batch:
            loads[i].start()

    barrier = pltpu.get_barrier_semaphore()
    for peer in far + near:
        pl.semaphore_signal(barrier, inc=1, device_id={"yz": peer}, device_id_type=MESH)

    @pl.when(gx > 0)
    def _():
        pl.semaphore_signal(barrier, inc=1, device_id={"gx": gx - 1}, device_id_type=MESH)

    @pl.when(gx < n_gx - 1)
    def _():
        pl.semaphore_signal(barrier, inc=1, device_id={"gx": gx + 1}, device_id_type=MESH)

    sides = (
        (0, 1, gx > 0, gx == 0, {"gx": gx - 1}),
        (1, 0, gx < n_gx - 1, gx == n_gx - 1, {"gx": gx + 1}),
        (2, 3, me > 0, me == 0, {"yz": me - 1}),
        (3, 2, me < n - 1, me == n - 1, {"yz": me + 1}),
    )
    def face_copy(side, other, where, send, recv, send_sem, recv_sem):
        return pltpu.make_async_remote_copy(
            src_ref=send.at[side],
            dst_ref=recv.at[other],
            send_sem=send_sem.at[1],
            recv_sem=recv_sem.at[0],
            device_id=where,
            device_id_type=MESH,
        )

    def faces_start(send, recv, send_sem, recv_sem):
        for side, other, there, edge, where in sides:

            @pl.when(there)
            def _(side=side, other=other, where=where):
                face_copy(side, other, where, send, recv, send_sem, recv_sem).start()

            @pl.when(edge)
            def _(side=side):
                pltpu.make_async_copy(
                    zeros.at[pl.ds(0, recv.shape[1])], recv.at[side], recv_sem.at[0]
                ).start()

    def faces_wait(send, recv, send_sem, recv_sem):
        arrived(math.prod(recv.shape[:-1]), v_ref, recv_sem.at[0])

    face_args = (face_send, face_recv, sent_s, face_r)
    stress_args = (stress_send, stress_recv, sent_s, stress_r)

    def all_copy(peer, source, send, recv, height, pitch, parts, send_sem, recv_sem):
        return pltpu.make_async_remote_copy(
            src_ref=send.at[pl.ds(pl.multiple_of(peer * pitch, 8), height), :],
            dst_ref=recv.at[pl.ds(pl.multiple_of(source * pitch, 8), height), :],
            send_sem=send_sem.at[0],
            recv_sem=recv_sem.at[lax.div(source * parts, n)],
            device_id={"yz": peer},
            device_id_type=MESH,
        )

    def all_start(peers, *args):
        for peer in peers:
            all_copy(peer, me, *args).start()

    def own_copy(send, recv, height, pitch, parts, send_sem, recv_sem):
        own = pl.ds(pl.multiple_of(me * pitch, 8), height)
        return pltpu.make_async_copy(send.at[own, :], recv.at[own, :], recv_sem.at[lax.div(me * parts, n)])

    def all_wait(part, send, recv, height, pitch, parts, send_sem, recv_sem):
        arrived(n // parts * height, v_ref, recv_sem.at[part])

    pay_args = (out_ref, in_ref, SENT * cap + 1, rows, 2, sent_s, out_r)
    back_args = (back_send, back_recv, 3 * cap, back_rows, 1, sent_s, back_r)

    def arrived(count, buffer, sem):
        rows = buffer.at[pl.ds(0, count), :]
        pltpu.make_async_copy(rows, rows, sem).wait()

    def landed(batch):
        arrived(sum(math.prod(held[i].shape[:-1]) for i in LOADS[batch]), v_ref, load_s.at[batch])

    zeros[...] = jnp.zeros(zeros.shape, F32)

    for batch in range(5):
        loads[LOADS[batch][0]].wait()
    iota = functools.partial(lax.broadcasted_iota, jnp.int32)

    def folded(shape, axis, period):
        place = iota(shape, axis)
        return jnp.where(place < period, place, place - period)

    eye = iota((moving, moving), 0) == iota((moving, moving), 1)
    target_row = target[...]
    target_col = jnp.sum(jnp.where(eye, target_row, 0), axis=1, keepdims=True)
    earlier = (target_col == target_row) & (iota((moving, moving), 0) < iota((moving, moving), 1))
    rank = jnp.sum(jnp.where(earlier, 1, 0), axis=0, keepdims=True)
    slot_row = rank * n + target_row
    slot_hot = onehot(folded((2 * received, moving), 0, received) == slot_row)
    block_hot = onehot(iota((blocks, moving), 0) == table[...]).astype(BF16)
    from_block = dot_last(slot_hot[:received].astype(BF16), block_hot).astype(BF16)
    from_twice = twice(from_block, 1)
    to_block = dot_last(block_hot, slot_hot.astype(BF16))
    moved = jnp.sum(to_block, axis=1, keepdims=True) > 0.5
    to_block = to_block.astype(BF16)
    pencil_out = jnp.sum(slot_hot[:received] * entered[...].astype(F32), axis=1, keepdims=True)

    home_t = onehot(folded((2 * pencils, blocks), 0, pencils) == home[...])
    home_hot = home_t.T.astype(BF16)
    home_t = twice(home_t[:pencils].astype(BF16), 1)
    live = onehot(iota((slots, blocks), 0) < tally[...]).T

    landed(5)
    u = [pick(home_hot, flow[c]) for c in range(3)]
    temp = pick(home_hot, heat[...])
    for c in range(4):
        grid = flow.at[c] if c < 3 else heat
        face_send[0, c] = grid[pl.ds(0, Y), :]
        face_send[1, c] = grid[pl.ds((X - 1) * Y, Y), :]
        face_send[2, c] = grid[pl.ds(0, X, stride=Y), :]
        face_send[3, c] = grid[pl.ds(Y - 1, X, stride=Y), :]

    where = cells[...]
    u = [lanes(u[c], where) for c in range(3)]
    spread = jnp.sqrt((1.0 - DECAY * DECAY) * lanes(temp, where))
    weight = mass[...] * live

    def send_row(c, value):
        for j in range(cap):
            out_ref[pl.ds(c * cap + j, n, stride=rows), :] = value[j * n : (j + 1) * n]

    send_row(6, pick(from_twice, weight))
    send_row(7, dot(from_block, where.astype(F32).astype(BF16)))
    place = lax.div(iota((n, slots), 1), slots // cap)
    pencil_row = jnp.broadcast_to(pencil_out[:n], (n, slots))
    for j in range(1, cap):
        pencil_row = jnp.where(place == j, pencil_out[j * n : (j + 1) * n], pencil_row)
    out_ref[pl.ds(SENT * cap, n, stride=rows), :] = pencil_row

    landed(6)
    for c in range(3):
        send_row(3 + c, pick(from_twice, noise[3 + c]))

    first = [drift(speed[c], u[c], spread, noise[c]) for c in range(3)]
    for c in range(3):
        send_row(c, pick(from_twice, first[c]))

    near_gx = jnp.where(gx > 0, 1, 0) + jnp.where(gx < n_gx - 1, 1, 0)
    neighbours = near_gx + jnp.where(me > 0, 1, 0) + jnp.where(me < n - 1, 1, 0)
    pl.semaphore_wait(barrier, n - 1 + near_gx)
    late = lax.rem(gx, 2) == 1

    @pl.when(jnp.logical_not(late))
    def _():
        all_start(far + near, *pay_args)

    faces_start(*face_args)
    own_copy(*pay_args).start()

    second = [drift(first[c], u[c], spread, noise[3 + c]) for c in range(3)]
    for c in range(3):
        second_ref[c] = second[c]
    put_terms(v_ref, blocks, jnp.where(moved, 0.0, weight), second)
    deposit(blocks, v_ref, cells, pb_ref)

    @pl.when(late)
    def _():
        all_start(far + near, *pay_args)
    for k in range(MOMENTS):
        moments[k] = pick(home_t, deposited(pb_ref, blocks, k))

    def migrants(side, base):
        def taken(row):
            return in_ref[pl.ds(base * rows + row, n // 2, stride=rows), :]

        got = [jnp.concatenate([taken(c * cap + j) for j in range(cap)], axis=0) for c in range(SENT)]
        where = got[7].astype(jnp.int32)
        cells_a[side] = where
        pencil_row = taken(SENT * cap)
        pencil = jnp.concatenate(
            [lanes(pencil_row, jnp.full((n // 2, slots), j * (slots // cap), jnp.int32)) for j in range(cap)], axis=0
        ).astype(jnp.int32)
        hot = onehot(pencil[:, : 2 * pencils] == folded((group, 2 * pencils), 1, pencils))
        narrow = hot[:, :pencils]
        hot = hot.astype(BF16)
        u = [lanes(pick(hot, flow[c]), where) for c in range(3)]
        spread = jnp.sqrt((1.0 - DECAY * DECAY) * lanes(pick(hot, heat[...]), where))
        second = [drift(got[c], u[c], spread, got[3 + c]) for c in range(3)]
        put_terms(v_ref.at[pl.ds(side * group // 2 * PAIR_PITCH, group // 2 * PAIR_PITCH), :], group, got[6], second)
        deposit(
            group,
            v_ref.at[pl.ds(side * group // 2 * PAIR_PITCH, group // 2 * PAIR_PITCH), :],
            cells_a.at[side],
            pb_ref.at[pl.ds(side * group // 2 * PITCH, group // 2 * PITCH), :],
        )
        return where, hot, narrow, second

    all_wait(half_a, *pay_args)
    where_n, hot_n, narrow_n, second_n = migrants(0, base_a)
    all_wait(half_b, *pay_args)
    where_f, hot_f, narrow_f, second_f = migrants(1, base_b)
    hot_t = twice(jnp.concatenate([narrow_n, narrow_f], axis=0), 0).T.astype(BF16)

    def total(k):
        parts = [
            deposited(pb_ref.at[pl.ds(side * group // 2 * PITCH, group // 2 * PITCH), :], group, k) for side in range(2)
        ]
        moments[k] = moments[k] + pick(hot_t, jnp.concatenate(parts, axis=0))

    for k in range(4, MOMENTS):
        total(k)
    for row in range(3):
        k = 4 + X_FACE[row]
        stress_send[0, row] = moments[k, pl.ds(0, Y), :]
        stress_send[1, row] = moments[k, pl.ds(pencils - Y, Y), :]
        k = 4 + Y_FACE[row]
        stress_send[2, row] = moments[k, pl.ds(0, X, stride=Y), :]
        stress_send[3, row] = moments[k, pl.ds(Y - 1, X, stride=Y), :]
    faces_start(*stress_args)
    for k in range(4):
        total(k)

    lane = iota((pencils, Z), 1)

    def along_z(x, step):
        if step > 0:
            return jnp.where(lane == Z - 1, 0.0, pltpu.roll(x, Z - 1, 1))
        return jnp.where(lane == 0, 0.0, pltpu.roll(x, 1, 1))

    def fill(slot, value):
        wide[slot, 1 : X + 1, 8 : 8 + Y, :] = value.reshape(X, Y, Z)

    def edge_x(slot, halo, c):
        wide[slot, 0, 8 : 8 + Y, :] = halo[0, c]
        wide[slot, X + 1, 8 : 8 + Y, :] = halo[1, c]

    def edge_y(slot, halo, c):
        for x in range(X):
            wide[slot, x + 1, 7:8, :] = halo[2, c, x : x + 1]
            wide[slot, x + 1, 8 + Y : 9 + Y, :] = halo[3, c, x : x + 1]

    def along_x(slot, step):
        return wide[slot, 1 + step : 1 + step + X, 8 : 8 + Y, :].reshape(pencils, Z)

    def along_y(slot, step):
        return wide[slot, 1 : X + 1, 8 + step : 8 + step + Y, :].reshape(pencils, Z)

    faces_wait(*face_args)
    f = [flow[0], flow[1], flow[2], heat[...]]
    base = []
    for c in range(4):
        fill(c, f[c])
        edge_x(c, face_recv, c)
        edge_y(c, face_recv, c)
        smooth = along_x(c, 1) + along_x(c, -1) + along_y(c, 1) + along_y(c, -1)
        smooth = smooth + along_z(f[c], 1) + along_z(f[c], -1) - 6.0 * f[c]
        base.append(f[c] + VISCOSITY * smooth)
    density = moments[0]
    momentum = [moments[1 + c] for c in range(3)]
    for c in range(3):
        base[c] = base[c] + COUPLING * (momentum[c] - density * f[c])
    dots = momentum[0] * f[0] + momentum[1] * f[1] + momentum[2] * f[2]
    squares = f[0] * f[0] + f[1] * f[1] + f[2] * f[2]
    energy = (moments[4] + moments[7] + moments[9] - 2.0 * dots + density * squares) / 3.0
    fields_out[3] = base[3] + COUPLING * (energy - density * f[3])
    stress = [moments[4 + s] for s in range(6)]
    for s in range(5):
        fill(4 + s, stress[s])
    for row in range(3):
        sz = stress[PAIR_INDEX[row][2]]
        base[row] = base[row] - (0.5 * STRESS_GAIN) * (along_z(sz, 1) - along_z(sz, -1))

    faces_wait(*stress_args)
    for row in range(3):
        edge_x(4 + X_FACE[row], stress_recv, row)
        edge_y(4 + Y_FACE[row], stress_recv, row)
    fresh = []
    for row in range(3):
        sx, sy = 4 + X_FACE[row], 4 + Y_FACE[row]
        slope = along_x(sx, 1) - along_x(sx, -1) + along_y(sy, 1) - along_y(sy, -1)
        value = base[row] - (0.5 * STRESS_GAIN) * slope
        fields_out[row] = value
        fresh.append(jnp.concatenate(split(value), axis=0))

    for base, where_a, hot, second_a in (
        (base_a, where_n, hot_n, second_n),
        (base_b, where_f, hot_f, second_f),
    ):
        for c in range(3):
            w = lanes(dot(hot, fresh[c]), where_a)
            third = second_a[c] + RELAXATION * (w - second_a[c])
            for j in range(cap):
                back_send[pl.ds(base * back_rows + c * cap + j, n // 2, stride=back_rows), :] = third[
                    j * (n // 2) : (j + 1) * (n // 2)
                ]
    all_start(others, *back_args)
    own_copy(*back_args).start()
    for c in range(3):
        w = lanes(dot(home_hot, fresh[c]), where)
        now = second_ref[c]
        second_ref[c] = live * (now + RELAXATION * (w - now))
    all_wait(0, *back_args)
    for c in range(3):
        returned = jnp.concatenate(
            [back_recv[pl.ds(c * cap + j, n, stride=back_rows), :] for j in range(cap)], axis=0
        )
        speed_out[c] = jnp.where(moved, live * pick(to_block, returned), second_ref[c])

    arrived((n - 1) * (pay_args[2] + back_args[2]), v_ref, sent_s.at[0])
    for count in range(1, 5):

        @pl.when(neighbours == count)
        def _(count=count):
            arrived(count * sum(math.prod(x.shape[1:-1]) for x in (face_send, stress_send)), v_ref, sent_s.at[1])


def put_out(fields, velocity, fields_out, velocity_out, sems):
    copies = (
        pltpu.make_async_copy(fields, fields_out, sems.at[0]),
        pltpu.make_async_copy(velocity, velocity_out, sems.at[1]),
    )
    for copy in copies:
        copy.start()
    for copy in copies:
        copy.wait()


def shards(
    flow_speed_field,
    thermal_field,
    walker_speed_vectors,
    walker_statistical_mass,
    gaussian_samples,
    walker_strip_position,
    group_active_tally,
    group_resident_strip,
    migrating_group_table,
    target_processor_slot,
    entered_strip_slot,
):
    n = lax.axis_size("yz")
    n_gx = lax.axis_size("gx")
    X, Y, Z = thermal_field.shape
    blocks, slots = walker_statistical_mass.shape
    moving = migrating_group_table.shape[0]
    cap = 2 * moving // n
    received = n * cap
    rows = -(-(SENT * cap + 1) // 8) * 8
    back_rows = -(-3 * cap // 8) * 8 + 8
    operands = (
        flow_speed_field.reshape(3, X * Y, Z),
        thermal_field.reshape(X * Y, Z),
        walker_speed_vectors,
        walker_statistical_mass,
        gaussian_samples.reshape(6, blocks, slots),
        walker_strip_position,
        group_active_tally.reshape(1, blocks),
        group_resident_strip.reshape(1, blocks),
        migrating_group_table.reshape(1, moving),
        target_processor_slot.reshape(1, moving),
        entered_strip_slot.reshape(1, moving),
    )
    vmem = pl.BlockSpec(memory_space=pltpu.VMEM)
    fields, velocity = pl.pallas_call(
        functools.partial(kernel, n, n_gx, (X, Y, Z)),
        out_shape=(
            pltpu.VMEM((4, X * Y, Z), F32),
            pltpu.VMEM((3, blocks, slots), F32),
        ),
        in_specs=[pl.BlockSpec(memory_space=pltpu.HBM)] * 11,
        out_specs=(vmem, vmem),
        scratch_shapes=[pltpu.VMEM(x.shape, x.dtype) for x in operands]
        + [pltpu.SemaphoreType.DMA((len(LOADS),))]
        + [
            pltpu.VMEM((max(blocks, received) // 2 * PAIR_PITCH, slots), F32),
            pltpu.VMEM((max(blocks, received) // 2 * PITCH, Z), F32),
            pltpu.VMEM((3, blocks, slots), F32),
            pltpu.VMEM((2, received // 2, slots), jnp.int32),
            pltpu.VMEM((MOMENTS, X * Y, Z), F32),
            pltpu.VMEM((9, X + 2, 24, Z), F32),
            pltpu.VMEM((4, 8, Z), F32),
            pltpu.VMEM((4, 4, 8, Z), F32),
            pltpu.VMEM((4, 4, 8, Z), F32),
            pltpu.VMEM((4, 3, 8, Z), F32),
            pltpu.VMEM((4, 3, 8, Z), F32),
            pltpu.VMEM((n * rows, slots), F32),
            pltpu.VMEM((n * rows, slots), F32),
            pltpu.VMEM((n * back_rows, slots), F32),
            pltpu.VMEM((n * back_rows, slots), F32),
            pltpu.SemaphoreType.DMA((2,)),
            pltpu.SemaphoreType.DMA((2,)),
            pltpu.SemaphoreType.DMA((1,)),
            pltpu.SemaphoreType.DMA((1,)),
            pltpu.SemaphoreType.DMA((1,)),
        ],
        compiler_params=pltpu.CompilerParams(
            collective_id=0, has_side_effects=True, vmem_limit_bytes=32 * 1024 * 1024
        ),
    )(*(pltpu.with_memory_space_constraint(x, pltpu.HBM) for x in operands))
    hbm = pl.BlockSpec(memory_space=pltpu.HBM)
    fields, velocity = pl.pallas_call(
        put_out,
        out_shape=(
            jax.ShapeDtypeStruct((4, X * Y, Z), F32),
            jax.ShapeDtypeStruct((3, blocks, slots), F32),
        ),
        in_specs=[vmem, vmem],
        out_specs=(hbm, hbm),
        scratch_shapes=[pltpu.SemaphoreType.DMA((2,))],
        compiler_params=pltpu.CompilerParams(vmem_limit_bytes=32 * 1024 * 1024),
    )(fields, velocity)
    return fields.reshape(4, X, Y, Z), velocity


def solution(mesh):
    return jax.shard_map(
        shards,
        mesh=mesh,
        in_specs=(
            P(None, "gx", "yz", None),
            P("gx", "yz", None),
            P(None, ("gx", "yz"), None),
            P(("gx", "yz"), None),
            P(None, None, ("gx", "yz"), None),
            P(("gx", "yz"), None),
            P(("gx", "yz")),
            P(("gx", "yz")),
            P(("gx", "yz")),
            P(("gx", "yz"), None),
            P(("gx", "yz")),
        ),
        out_specs=(P(None, "gx", "yz", None), P(None, ("gx", "yz"), None)),
        check_vma=False,
    )
```

```python
import functools
import math

import jax
import jax.numpy as jnp
from jax import lax
from jax.experimental import pallas as pl
from jax.experimental.pallas import tpu as pltpu
from jax.sharding import PartitionSpec as P

DECAY = 0.6
VISCOSITY = 0.05
COUPLING = 0.02
STRESS_GAIN = 0.005
RELAXATION = 0.5
PAIRS = ((0, 0), (0, 1), (0, 2), (1, 1), (1, 2), (2, 2))
PAIR_INDEX = ((0, 1, 2), (1, 3, 4), (2, 4, 5))
MOMENTS = 10
PITCH = 24
PAIR_PITCH = 56
SENT = 8
UNROLL = 16
LOADS = ((8,), (9,), (10,), (7,), (6,), (0, 1, 5, 3), (4, 2))
X_FACE = tuple(row[0] for row in PAIR_INDEX)
Y_FACE = tuple(row[1] for row in PAIR_INDEX)
MESH = pl.DeviceIdType.MESH
BF16 = jnp.bfloat16
F32 = jnp.float32


def split(x):
    high = x.astype(BF16)
    return high, (x - high.astype(F32)).astype(BF16)


def dot(a, b):
    return jnp.dot(a, b, preferred_element_type=F32)


def dot_last(a, b):
    return lax.dot_general(a, b, (((1,), (1,)), ((), ())), preferred_element_type=F32)


def twice(x, axis):
    return jnp.concatenate([x, x], axis=axis)


def pick(onehot_twice, x):
    return dot(onehot_twice, jnp.concatenate(split(x), axis=0))


def lanes(x, index):
    return jnp.take_along_axis(x, index, axis=1, mode="promise_in_bounds")


def onehot(condition):
    return jnp.where(condition, 1.0, 0.0)


def partner(me, i, n):
    peer, bit = 0, 1
    while bit < n:
        own = lax.rem(lax.div(me, bit), 2)
        peer = peer + bit * (1 - own if i & bit else own)
        bit *= 2
    return peer


def drift(start, u, spread, noise):
    return u + DECAY * (start - u) + spread * noise


def deposit(count, v_ref, cells_ref, pb_ref):
    width = v_ref.shape[1]
    slots = cells_ref.shape[1]
    half = count // 2
    unroll = math.gcd(half, UNROLL)
    where = lax.broadcasted_iota(jnp.int32, (width, slots), 0)
    none = jnp.zeros((8, slots), F32)
    mine = lax.broadcasted_iota(jnp.int32, (8, slots), 0) < MOMENTS - 8

    def some(step, carry):
        for t in range(unroll):
            n = step * unroll + t
            start = pl.multiple_of(n * PAIR_PITCH, 8)
            rows = [v_ref[pl.ds(start + 8 * part, 8), :] for part in range(6)]
            left = [rows[0], jnp.where(mine, rows[1], 0.0), none, rows[3], jnp.where(mine, rows[4], 0.0), none]
            right = [none, jnp.where(mine, 0.0, rows[1]), rows[2], none, jnp.where(mine, 0.0, rows[4]), rows[5]]
            lhs = jnp.concatenate(
                [jnp.concatenate(side, axis=0).astype(BF16) for side in (left, right)], axis=1
            )
            hot = jnp.concatenate(
                [onehot(cells_ref[pl.ds(n + block, 1), :] == where).astype(BF16) for block in (0, half)], axis=1
            )
            out = dot_last(lhs, hot)
            pb_ref[pl.ds(pl.multiple_of(n * PITCH, 8), PITCH), :] = out[:PITCH] + out[PITCH:]
        return carry

    lax.fori_loop(0, half // unroll, some, 0)


def put_terms(v_ref, count, weight, second):
    half = count // 2
    weighted = [weight * second[row] for row in range(3)]
    terms = [weight] + weighted + [weighted[one] * second[two] for one, two in PAIRS]
    for k, term in enumerate(terms):
        high = term.astype(BF16).astype(F32)
        for part, value in enumerate((high, term - high)):
            for block in range(2):
                v_ref[pl.ds(part * PITCH + block * MOMENTS + k, half, stride=PAIR_PITCH), :] = value[
                    block * half : (block + 1) * half
                ]


def deposited(pb_ref, count, k):
    half = count // 2
    return jnp.concatenate(
        [pb_ref[pl.ds(block * MOMENTS + k, half, stride=PITCH), :] for block in range(2)], axis=0
    )


def kernel(
    n,
    n_gx,
    spans,
    *refs,
):
    sources, results, held, load_s = refs[:11], refs[11:16], refs[16:27], refs[27]
    fields_out, speed_out, returned_out, to_block_out, live_out = results
    flow, heat, speed, mass, noise, cells, tally, home, table, target, entered = held
    (
    v_ref,
    pb_ref,
    second_ref,
    cells_a,
    moments,
    wide,
    zeros,
    face_send,
    face_recv,
    stress_send,
    stress_recv,
    out_ref,
    in_ref,
    back_send,
    back_recv,
    sent_s,
    out_r,
    face_r,
    stress_r,
    back_r,
    ) = refs[28:]
    loads = [
        pltpu.make_async_copy(source, kept, load_s.at[[i in batch for batch in LOADS].index(True)])
        for i, (source, kept) in enumerate(zip(sources, held))
    ]
    X, Y, Z = spans
    pencils = X * Y
    blocks, slots = mass.shape
    moving = table.shape[1]
    cap = 2 * moving // n
    received = n * cap
    rows = out_ref.shape[0] // n
    back_rows = back_send.shape[0] // n
    gx = lax.axis_index("gx")
    me = lax.axis_index("yz")
    far = [partner(me, i, n) for i in range(n - 1, n // 2 - 1, -1)]
    near = [partner(me, i, n) for i in range(n // 2 - 1, 0, -1)]
    odd = lax.rem(gx, 2)
    turns = [j + odd * (n - 2 - 2 * j) for j in range(n - 1)]
    others = [j + lax.div(j + n - me, n) for j in turns]
    group = received // 2
    half_a = jnp.minimum(lax.div(me, n // 4), 1)
    half_b = 1 - half_a
    base_a, base_b = half_a * (n // 2), half_b * (n // 2)
    for batch in LOADS:
        for i in batch:
            loads[i].start()

    barrier = pltpu.get_barrier_semaphore()
    for peer in far + near:
        pl.semaphore_signal(barrier, inc=1, device_id={"yz": peer}, device_id_type=MESH)

    @pl.when(gx > 0)
    def _():
        pl.semaphore_signal(barrier, inc=1, device_id={"gx": gx - 1}, device_id_type=MESH)

    @pl.when(gx < n_gx - 1)
    def _():
        pl.semaphore_signal(barrier, inc=1, device_id={"gx": gx + 1}, device_id_type=MESH)

    sides = (
        (0, 1, gx > 0, gx == 0, {"gx": gx - 1}),
        (1, 0, gx < n_gx - 1, gx == n_gx - 1, {"gx": gx + 1}),
        (2, 3, me > 0, me == 0, {"yz": me - 1}),
        (3, 2, me < n - 1, me == n - 1, {"yz": me + 1}),
    )
    def face_copy(side, other, where, send, recv, send_sem, recv_sem):
        return pltpu.make_async_remote_copy(
            src_ref=send.at[side],
            dst_ref=recv.at[other],
            send_sem=send_sem.at[1],
            recv_sem=recv_sem.at[0],
            device_id=where,
            device_id_type=MESH,
        )

    def faces_start(send, recv, send_sem, recv_sem):
        for side, other, there, edge, where in sides:

            @pl.when(there)
            def _(side=side, other=other, where=where):
                face_copy(side, other, where, send, recv, send_sem, recv_sem).start()

            @pl.when(edge)
            def _(side=side):
                pltpu.make_async_copy(
                    zeros.at[pl.ds(0, recv.shape[1])], recv.at[side], recv_sem.at[0]
                ).start()

    def faces_wait(send, recv, send_sem, recv_sem):
        arrived(math.prod(recv.shape[:-1]), v_ref, recv_sem.at[0])

    face_args = (face_send, face_recv, sent_s, face_r)
    stress_args = (stress_send, stress_recv, sent_s, stress_r)

    def all_copy(peer, source, send, recv, height, pitch, parts, send_sem, recv_sem):
        return pltpu.make_async_remote_copy(
            src_ref=send.at[pl.ds(pl.multiple_of(peer * pitch, 8), height), :],
            dst_ref=recv.at[pl.ds(pl.multiple_of(source * pitch, 8), height), :],
            send_sem=send_sem.at[0],
            recv_sem=recv_sem.at[lax.div(source * parts, n)],
            device_id={"yz": peer},
            device_id_type=MESH,
        )

    def all_start(peers, *args):
        for peer in peers:
            all_copy(peer, me, *args).start()

    def own_copy(send, recv, height, pitch, parts, send_sem, recv_sem):
        own = pl.ds(pl.multiple_of(me * pitch, 8), height)
        return pltpu.make_async_copy(send.at[own, :], recv.at[own, :], recv_sem.at[lax.div(me * parts, n)])

    def all_wait(part, send, recv, height, pitch, parts, send_sem, recv_sem):
        arrived(n // parts * height, v_ref, recv_sem.at[part])

    pay_args = (out_ref, in_ref, SENT * cap + 1, rows, 2, sent_s, out_r)
    back_args = (back_send, back_recv, 3 * cap, back_rows, 1, sent_s, back_r)

    def arrived(count, buffer, sem):
        rows = buffer.at[pl.ds(0, count), :]
        pltpu.make_async_copy(rows, rows, sem).wait()

    def landed(batch):
        arrived(sum(math.prod(held[i].shape[:-1]) for i in LOADS[batch]), v_ref, load_s.at[batch])

    zeros[...] = jnp.zeros(zeros.shape, F32)

    for batch in range(5):
        loads[LOADS[batch][0]].wait()
    iota = functools.partial(lax.broadcasted_iota, jnp.int32)

    def folded(shape, axis, period):
        place = iota(shape, axis)
        return jnp.where(place < period, place, place - period)

    eye = iota((moving, moving), 0) == iota((moving, moving), 1)
    target_row = target[...]
    target_col = jnp.sum(jnp.where(eye, target_row, 0), axis=1, keepdims=True)
    earlier = (target_col == target_row) & (iota((moving, moving), 0) < iota((moving, moving), 1))
    rank = jnp.sum(jnp.where(earlier, 1, 0), axis=0, keepdims=True)
    slot_row = rank * n + target_row
    slot_hot = onehot(folded((2 * received, moving), 0, received) == slot_row)
    block_hot = onehot(iota((blocks, moving), 0) == table[...]).astype(BF16)
    from_block = dot_last(slot_hot[:received].astype(BF16), block_hot).astype(BF16)
    from_twice = twice(from_block, 1)
    to_block = dot_last(block_hot, slot_hot.astype(BF16))
    moved = jnp.sum(to_block, axis=1, keepdims=True) > 0.5
    to_block = to_block.astype(BF16)
    pencil_out = jnp.sum(slot_hot[:received] * entered[...].astype(F32), axis=1, keepdims=True)

    home_t = onehot(folded((2 * pencils, blocks), 0, pencils) == home[...])
    home_hot = home_t.T.astype(BF16)
    home_t = twice(home_t[:pencils].astype(BF16), 1)
    live = onehot(iota((slots, blocks), 0) < tally[...]).T

    landed(5)
    u = [pick(home_hot, flow[c]) for c in range(3)]
    temp = pick(home_hot, heat[...])
    for c in range(4):
        grid = flow.at[c] if c < 3 else heat
        face_send[0, c] = grid[pl.ds(0, Y), :]
        face_send[1, c] = grid[pl.ds((X - 1) * Y, Y), :]
        face_send[2, c] = grid[pl.ds(0, X, stride=Y), :]
        face_send[3, c] = grid[pl.ds(Y - 1, X, stride=Y), :]

    where = cells[...]
    u = [lanes(u[c], where) for c in range(3)]
    spread = jnp.sqrt((1.0 - DECAY * DECAY) * lanes(temp, where))
    weight = mass[...] * live

    def send_row(c, value):
        for j in range(cap):
            out_ref[pl.ds(c * cap + j, n, stride=rows), :] = value[j * n : (j + 1) * n]

    send_row(6, pick(from_twice, weight))
    send_row(7, dot(from_block, where.astype(F32).astype(BF16)))
    place = lax.div(iota((n, slots), 1), slots // cap)
    pencil_row = jnp.broadcast_to(pencil_out[:n], (n, slots))
    for j in range(1, cap):
        pencil_row = jnp.where(place == j, pencil_out[j * n : (j + 1) * n], pencil_row)
    out_ref[pl.ds(SENT * cap, n, stride=rows), :] = pencil_row

    landed(6)
    for c in range(3):
        send_row(3 + c, pick(from_twice, noise[3 + c]))

    first = [drift(speed[c], u[c], spread, noise[c]) for c in range(3)]
    for c in range(3):
        send_row(c, pick(from_twice, first[c]))

    near_gx = jnp.where(gx > 0, 1, 0) + jnp.where(gx < n_gx - 1, 1, 0)
    neighbours = near_gx + jnp.where(me > 0, 1, 0) + jnp.where(me < n - 1, 1, 0)
    pl.semaphore_wait(barrier, n - 1 + near_gx)
    late = lax.rem(gx, 2) == 1

    @pl.when(jnp.logical_not(late))
    def _():
        all_start(far + near, *pay_args)

    faces_start(*face_args)
    own_copy(*pay_args).start()

    second = [drift(first[c], u[c], spread, noise[3 + c]) for c in range(3)]
    for c in range(3):
        second_ref[c] = second[c]
    put_terms(v_ref, blocks, jnp.where(moved, 0.0, weight), second)
    deposit(blocks, v_ref, cells, pb_ref)

    @pl.when(late)
    def _():
        all_start(far + near, *pay_args)
    for k in range(MOMENTS):
        moments[k] = pick(home_t, deposited(pb_ref, blocks, k))

    def migrants(side, base):
        def taken(row):
            return in_ref[pl.ds(base * rows + row, n // 2, stride=rows), :]

        got = [jnp.concatenate([taken(c * cap + j) for j in range(cap)], axis=0) for c in range(SENT)]
        where = got[7].astype(jnp.int32)
        cells_a[side] = where
        pencil_row = taken(SENT * cap)
        pencil = jnp.concatenate(
            [lanes(pencil_row, jnp.full((n // 2, slots), j * (slots // cap), jnp.int32)) for j in range(cap)], axis=0
        ).astype(jnp.int32)
        hot = onehot(pencil[:, : 2 * pencils] == folded((group, 2 * pencils), 1, pencils))
        narrow = hot[:, :pencils]
        hot = hot.astype(BF16)
        u = [lanes(pick(hot, flow[c]), where) for c in range(3)]
        spread = jnp.sqrt((1.0 - DECAY * DECAY) * lanes(pick(hot, heat[...]), where))
        second = [drift(got[c], u[c], spread, got[3 + c]) for c in range(3)]
        put_terms(v_ref.at[pl.ds(side * group // 2 * PAIR_PITCH, group // 2 * PAIR_PITCH), :], group, got[6], second)
        deposit(
            group,
            v_ref.at[pl.ds(side * group // 2 * PAIR_PITCH, group // 2 * PAIR_PITCH), :],
            cells_a.at[side],
            pb_ref.at[pl.ds(side * group // 2 * PITCH, group // 2 * PITCH), :],
        )
        return where, hot, narrow, second

    all_wait(half_a, *pay_args)
    where_n, hot_n, narrow_n, second_n = migrants(0, base_a)
    all_wait(half_b, *pay_args)
    where_f, hot_f, narrow_f, second_f = migrants(1, base_b)
    hot_t = twice(jnp.concatenate([narrow_n, narrow_f], axis=0), 0).T.astype(BF16)

    def total(k):
        parts = [
            deposited(pb_ref.at[pl.ds(side * group // 2 * PITCH, group // 2 * PITCH), :], group, k) for side in range(2)
        ]
        moments[k] = moments[k] + pick(hot_t, jnp.concatenate(parts, axis=0))

    for k in range(4, MOMENTS):
        total(k)
    for row in range(3):
        k = 4 + X_FACE[row]
        stress_send[0, row] = moments[k, pl.ds(0, Y), :]
        stress_send[1, row] = moments[k, pl.ds(pencils - Y, Y), :]
        k = 4 + Y_FACE[row]
        stress_send[2, row] = moments[k, pl.ds(0, X, stride=Y), :]
        stress_send[3, row] = moments[k, pl.ds(Y - 1, X, stride=Y), :]
    faces_start(*stress_args)
    for k in range(4):
        total(k)

    lane = iota((pencils, Z), 1)

    def along_z(x, step):
        if step > 0:
            return jnp.where(lane == Z - 1, 0.0, pltpu.roll(x, Z - 1, 1))
        return jnp.where(lane == 0, 0.0, pltpu.roll(x, 1, 1))

    def fill(slot, value):
        wide[slot, 1 : X + 1, 8 : 8 + Y, :] = value.reshape(X, Y, Z)

    def edge_x(slot, halo, c):
        wide[slot, 0, 8 : 8 + Y, :] = halo[0, c]
        wide[slot, X + 1, 8 : 8 + Y, :] = halo[1, c]

    def edge_y(slot, halo, c):
        for x in range(X):
            wide[slot, x + 1, 7:8, :] = halo[2, c, x : x + 1]
            wide[slot, x + 1, 8 + Y : 9 + Y, :] = halo[3, c, x : x + 1]

    def along_x(slot, step):
        return wide[slot, 1 + step : 1 + step + X, 8 : 8 + Y, :].reshape(pencils, Z)

    def along_y(slot, step):
        return wide[slot, 1 : X + 1, 8 + step : 8 + step + Y, :].reshape(pencils, Z)

    faces_wait(*face_args)
    f = [flow[0], flow[1], flow[2], heat[...]]
    base = []
    for c in range(4):
        fill(c, f[c])
        edge_x(c, face_recv, c)
        edge_y(c, face_recv, c)
        smooth = along_x(c, 1) + along_x(c, -1) + along_y(c, 1) + along_y(c, -1)
        smooth = smooth + along_z(f[c], 1) + along_z(f[c], -1) - 6.0 * f[c]
        base.append(f[c] + VISCOSITY * smooth)
    density = moments[0]
    momentum = [moments[1 + c] for c in range(3)]
    for c in range(3):
        base[c] = base[c] + COUPLING * (momentum[c] - density * f[c])
    dots = momentum[0] * f[0] + momentum[1] * f[1] + momentum[2] * f[2]
    squares = f[0] * f[0] + f[1] * f[1] + f[2] * f[2]
    energy = (moments[4] + moments[7] + moments[9] - 2.0 * dots + density * squares) / 3.0
    fields_out[3] = base[3] + COUPLING * (energy - density * f[3])
    stress = [moments[4 + s] for s in range(6)]
    for s in range(5):
        fill(4 + s, stress[s])
    for row in range(3):
        sz = stress[PAIR_INDEX[row][2]]
        base[row] = base[row] - (0.5 * STRESS_GAIN) * (along_z(sz, 1) - along_z(sz, -1))

    faces_wait(*stress_args)
    for row in range(3):
        edge_x(4 + X_FACE[row], stress_recv, row)
        edge_y(4 + Y_FACE[row], stress_recv, row)
    fresh = []
    for row in range(3):
        sx, sy = 4 + X_FACE[row], 4 + Y_FACE[row]
        slope = along_x(sx, 1) - along_x(sx, -1) + along_y(sy, 1) - along_y(sy, -1)
        value = base[row] - (0.5 * STRESS_GAIN) * slope
        fields_out[row] = value
        fresh.append(jnp.concatenate(split(value), axis=0))

    for base, where_a, hot, second_a in (
        (base_a, where_n, hot_n, second_n),
        (base_b, where_f, hot_f, second_f),
    ):
        for c in range(3):
            w = lanes(dot(hot, fresh[c]), where_a)
            third = second_a[c] + RELAXATION * (w - second_a[c])
            for j in range(cap):
                back_send[pl.ds(base * back_rows + c * cap + j, n // 2, stride=back_rows), :] = third[
                    j * (n // 2) : (j + 1) * (n // 2)
                ]
    all_start(others, *back_args)
    own_copy(*back_args).start()
    for c in range(3):
        w = lanes(dot(home_hot, fresh[c]), where)
        now = second_ref[c]
        speed_out[c] = jnp.where(moved, 0.0, live * (now + RELAXATION * (w - now)))
    to_block_out[...] = to_block
    live_out[...] = live
    all_wait(0, *back_args)
    for c in range(3):
        returned_out[c] = jnp.concatenate(
            [back_recv[pl.ds(c * cap + j, n, stride=back_rows), :] for j in range(cap)], axis=0
        )

    arrived((n - 1) * (pay_args[2] + back_args[2]), v_ref, sent_s.at[0])
    for count in range(1, 5):

        @pl.when(neighbours == count)
        def _(count=count):
            arrived(count * sum(math.prod(x.shape[1:-1]) for x in (face_send, stress_send)), v_ref, sent_s.at[1])


def put_out(fields, velocity, returned, to_block, live, fields_out, velocity_out, whole, sems):
    copies = [pltpu.make_async_copy(fields, fields_out, sems.at[3])]
    copies[0].start()
    for c in range(3):
        whole[c] = velocity[c] + live[...] * pick(to_block[...], returned[c])
        copies.append(pltpu.make_async_copy(whole.at[c], velocity_out.at[c], sems.at[c]))
        copies[-1].start()
    for copy in copies:
        copy.wait()


def shards(
    flow_speed_field,
    thermal_field,
    walker_speed_vectors,
    walker_statistical_mass,
    gaussian_samples,
    walker_strip_position,
    group_active_tally,
    group_resident_strip,
    migrating_group_table,
    target_processor_slot,
    entered_strip_slot,
):
    n = lax.axis_size("yz")
    n_gx = lax.axis_size("gx")
    X, Y, Z = thermal_field.shape
    blocks, slots = walker_statistical_mass.shape
    moving = migrating_group_table.shape[0]
    cap = 2 * moving // n
    received = n * cap
    rows = -(-(SENT * cap + 1) // 8) * 8
    back_rows = -(-3 * cap // 8) * 8 + 8
    operands = (
        flow_speed_field.reshape(3, X * Y, Z),
        thermal_field.reshape(X * Y, Z),
        walker_speed_vectors,
        walker_statistical_mass,
        gaussian_samples.reshape(6, blocks, slots),
        walker_strip_position,
        group_active_tally.reshape(1, blocks),
        group_resident_strip.reshape(1, blocks),
        migrating_group_table.reshape(1, moving),
        target_processor_slot.reshape(1, moving),
        entered_strip_slot.reshape(1, moving),
    )
    vmem = pl.BlockSpec(memory_space=pltpu.VMEM)
    parts = pl.pallas_call(
        functools.partial(kernel, n, n_gx, (X, Y, Z)),
        out_shape=(
            pltpu.VMEM((4, X * Y, Z), F32),
            pltpu.VMEM((3, blocks, slots), F32),
            pltpu.VMEM((3, received, slots), F32),
            pltpu.VMEM((blocks, 2 * received), BF16),
            pltpu.VMEM((blocks, slots), F32),
        ),
        in_specs=[pl.BlockSpec(memory_space=pltpu.HBM)] * 11,
        out_specs=(vmem,) * 5,
        scratch_shapes=[pltpu.VMEM(x.shape, x.dtype) for x in operands]
        + [pltpu.SemaphoreType.DMA((len(LOADS),))]
        + [
            pltpu.VMEM((max(blocks, received) // 2 * PAIR_PITCH, slots), F32),
            pltpu.VMEM((max(blocks, received) // 2 * PITCH, Z), F32),
            pltpu.VMEM((3, blocks, slots), F32),
            pltpu.VMEM((2, received // 2, slots), jnp.int32),
            pltpu.VMEM((MOMENTS, X * Y, Z), F32),
            pltpu.VMEM((9, X + 2, 24, Z), F32),
            pltpu.VMEM((4, 8, Z), F32),
            pltpu.VMEM((4, 4, 8, Z), F32),
            pltpu.VMEM((4, 4, 8, Z), F32),
            pltpu.VMEM((4, 3, 8, Z), F32),
            pltpu.VMEM((4, 3, 8, Z), F32),
            pltpu.VMEM((n * rows, slots), F32),
            pltpu.VMEM((n * rows, slots), F32),
            pltpu.VMEM((n * back_rows, slots), F32),
            pltpu.VMEM((n * back_rows, slots), F32),
            pltpu.SemaphoreType.DMA((2,)),
            pltpu.SemaphoreType.DMA((2,)),
            pltpu.SemaphoreType.DMA((1,)),
            pltpu.SemaphoreType.DMA((1,)),
            pltpu.SemaphoreType.DMA((1,)),
        ],
        compiler_params=pltpu.CompilerParams(
            collective_id=0, has_side_effects=True, vmem_limit_bytes=32 * 1024 * 1024
        ),
    )(*(pltpu.with_memory_space_constraint(x, pltpu.HBM) for x in operands))
    hbm = pl.BlockSpec(memory_space=pltpu.HBM)
    fields, velocity = pl.pallas_call(
        put_out,
        out_shape=(
            jax.ShapeDtypeStruct((4, X * Y, Z), F32),
            jax.ShapeDtypeStruct((3, blocks, slots), F32),
        ),
        in_specs=[vmem] * 5,
        out_specs=(hbm, hbm),
        scratch_shapes=[pltpu.VMEM((3, blocks, slots), F32), pltpu.SemaphoreType.DMA((4,))],
        compiler_params=pltpu.CompilerParams(vmem_limit_bytes=32 * 1024 * 1024),
    )(*parts)
    return fields.reshape(4, X, Y, Z), velocity


def solution(mesh):
    return jax.shard_map(
        shards,
        mesh=mesh,
        in_specs=(
            P(None, "gx", "yz", None),
            P("gx", "yz", None),
            P(None, ("gx", "yz"), None),
            P(("gx", "yz"), None),
            P(None, None, ("gx", "yz"), None),
            P(("gx", "yz"), None),
            P(("gx", "yz")),
            P(("gx", "yz")),
            P(("gx", "yz")),
            P(("gx", "yz"), None),
            P(("gx", "yz")),
        ),
        out_specs=(P(None, "gx", "yz", None), P(None, ("gx", "yz"), None)),
        check_vma=False,
    )
```
